256 devices in a mesh: role: 2 (over core), exp: 8 (over z), tp: 16 (over x, y).
Axes of the slice: x: 4, y: 4, z: 8, core: 2. Of those that a mesh axis runs over, the one named last changes fastest.
Arguments:
- residual_in: bfloat16 [2048, 8192], P(('role', 'exp', 'tp')), may hold values from -64 to 64
- context: bfloat16 [2048, 8192], P(('role', 'exp'), 'tp'), may hold values from -6 to 6
- out_weight: bfloat16 [8192, 8192], P('tp', ('role', 'exp')), may hold values from -0.0625 to 0.0625
- norm_gain: bfloat16 [8192], replicated, may hold values from 0.5 to 1.5
- router: bfloat16 [2, 4, 8192], replicated, may hold values from -0.125 to 0.125
- up_weight: bfloat16 [2, 8, 8192, 6144], P('role', 'exp', None, 'tp'), may hold values from -0.0625 to 0.0625
- down_weight: bfloat16 [2, 8, 6144, 8192], P('role', 'exp', 'tp'), may hold values from -0.109375 to 0.109375
- modality: int32 [2048], P(('role', 'exp', 'tp')), may hold values from 0 to 1
- expert: int32 [2048], P(('role', 'exp', 'tp')), may hold values from 0 to 3, as said below
Outputs:
- mixed: bfloat16 [2048, 8192], P(('role', 'exp', 'tp'))
The draws below stay inside these ranges and needn't reach their ends.
Inputs may be any that keep to these rules, and one draw needn't show every extreme that they name: Among the 8 tokens of one device at most 2 choose one expert of one modality, and in every device's tokens some expert of some modality is chosen by exactly 2.
All inputs are finite; a program needn't handle non-finite values.
Results may differ from the reference program's by a relative error of at most 0.0052.
Values may be sent and summed in bfloat16 or wider, within the bound.
A program may use at most 128 MiB of HBM per device.

```python
import jax
import jax.numpy as jnp
from jax import lax

D = 8192
FF = 12288
EXPERTS = 4
TOK_DEV = 8
CAP = 2
SPLIT = 2
TOKENS = 2048


def route_table(key):
    base = jax.random.fold_in(key, 7)
    blocks = TOKENS // TOK_DEV
    pool_size = 2 * EXPERTS * CAP

    def one_block(block_key):
        kind_key, noise_key, favor_key, order_key = jax.random.split(block_key, 4)
        block_kind = jax.random.randint(kind_key, (), 0, 4)
        slot_ids = jnp.arange(pool_size, dtype=jnp.int32)
        composite = slot_ids // CAP
        modal_of = composite // EXPERTS
        favored = jax.random.randint(favor_key, (), 0, 2 * EXPERTS)
        noise_part = jax.random.randint(noise_key, (pool_size,), 0, 65536) * pool_size + slot_ids
        penalty = jnp.where(block_kind < 2, (modal_of == 0).astype(jnp.int32), jnp.where(block_kind == 2, (modal_of == 1).astype(jnp.int32), (composite != favored).astype(jnp.int32)))
        scores = noise_part + penalty * 16777216
        picked = composite[jnp.argsort(scores)[:TOK_DEV]]
        return picked[jax.random.permutation(order_key, TOK_DEV)]
    routed = jax.vmap(one_block)(jax.random.split(base, blocks))
    return routed.reshape(TOKENS).astype(jnp.int32)


def draw_modality(key, part):
    return (route_table(key) // EXPERTS).astype(jnp.int32)


def draw_expert(key, part):
    return (route_table(key) % EXPERTS).astype(jnp.int32)


def draw_residual_in(key, part):
    row_key, col_key, value_key = jax.random.split(jax.random.fold_in(key, 11), 3)
    row_scale = jnp.exp(jax.random.uniform(row_key, (TOKENS, 1), jnp.float32, -1.15, 1.15))
    col_scale = jnp.exp(jax.random.uniform(col_key, (1, D), jnp.float32, -1.15, 1.15))
    values = jnp.clip(jax.random.normal(value_key, (TOKENS, D), jnp.float32), -6.0, 6.0)
    return (values * row_scale * col_scale).astype(jnp.bfloat16)


def level_of(stream_key, dims, shards, least, high):
    gain, own = 1.0, jax.random.fold_in(stream_key, 6)
    for axis_at, blocks in shards:
        heights = jnp.exp(jax.random.uniform(jax.random.fold_in(own, axis_at), (blocks,), jnp.float32, least / len(shards), high / len(shards)))
        gain = gain * jnp.repeat(heights, dims[axis_at] // blocks).reshape([-1 if axis == axis_at else 1 for axis in range(len(dims))])
    return gain


def gaussian(rng, shape, deviation, limit, cuts=(), kind=jnp.bfloat16):
    level = level_of(rng, shape, cuts, -0.22, 0.18) if cuts else 1.0
    values = jax.random.normal(rng, shape, jnp.float32) * deviation * level
    return jnp.minimum(jnp.maximum(values, -limit), limit).astype(kind)


def setup_inputs(seed: int = 0) -> dict:
    keys = jax.random.split(jax.random.key(seed), 10)
    residual_in = draw_residual_in(jax.random.fold_in(keys[9], 71), 0)
    context = gaussian(keys[1], (TOKENS, D), 1.0, 6.0, ((0, 16), (1, 16)))
    out_weight = gaussian(keys[2], (D, D), D ** -0.5, 0.0625, ((0, 16), (1, 16)))
    norm_gain = jnp.clip(1.0 + 0.1 * jax.random.normal(keys[3], (D,), jnp.float32), 0.5, 1.5).astype(jnp.bfloat16)
    router = gaussian(keys[4], (2, EXPERTS, D), (D // 4) ** -0.5, 0.125)
    up_weight = gaussian(keys[5], (2, EXPERTS * SPLIT, D, FF // SPLIT), D ** -0.5, 0.0625, ((0, 2), (1, 8), (3, 16)))
    down_weight = gaussian(keys[6], (2, EXPERTS * SPLIT, FF // SPLIT, D), (FF // 4) ** -0.5, 0.109375, ((0, 2), (1, 8), (2, 16)))
    modality = draw_modality(jax.random.fold_in(keys[9], 71), 0)
    expert = draw_expert(jax.random.fold_in(keys[9], 71), 0)
    return dict(residual_in=residual_in, context=context, out_weight=out_weight, norm_gain=norm_gain, router=router, up_weight=up_weight, down_weight=down_weight, modality=modality, expert=expert)


EPSILON = 1e-05

def reference(residual_in, context, out_weight, norm_gain, router, up_weight, down_weight, modality, expert):
    projected = jnp.dot(context, out_weight, preferred_element_type=jnp.float32)
    resid = (residual_in.astype(jnp.float32) + projected).astype(jnp.bfloat16)
    resid = lax.optimization_barrier(resid)
    widened = resid.astype(jnp.float32)
    inverse_rms = lax.rsqrt(lax.optimization_barrier(jnp.mean(widened * widened, axis=-1, keepdims=True)) + EPSILON)
    normed = (widened * inverse_rms * norm_gain.astype(jnp.float32)).astype(jnp.bfloat16)
    routes = (modality * EXPERTS + expert).astype(jnp.int32)
    router_rows = router.reshape(2 * EXPERTS, D)
    picked = jnp.take(router_rows, routes, axis=0).astype(jnp.float32)
    gating = jax.nn.sigmoid(lax.optimization_barrier(jnp.sum(normed.astype(jnp.float32) * picked, axis=-1)))
    up_split = up_weight.reshape(2 * EXPERTS, SPLIT, D, FF // SPLIT)
    down_full = down_weight.reshape(2 * EXPERTS, FF, D)
    row_limit = TOKENS // 4

    def one_route(running, route_id):
        chosen = jnp.argsort((routes != route_id).astype(jnp.int32), stable=True)[:row_limit].astype(jnp.int32)
        matched = jnp.sum((routes == route_id).astype(jnp.int32))
        in_range = jnp.arange(row_limit, dtype=jnp.int32) < matched
        inputs = jnp.take(normed, chosen, axis=0)
        up_parts = lax.dynamic_index_in_dim(up_split, route_id, 0, keepdims=False)
        up_matrix = jnp.transpose(up_parts, (1, 0, 2)).reshape(D, FF)
        down_matrix = lax.dynamic_index_in_dim(down_full, route_id, 0, keepdims=False)
        up_sums = jnp.dot(inputs, up_matrix, preferred_element_type=jnp.float32)
        hidden = jax.nn.gelu(up_sums).astype(jnp.bfloat16)
        result = jnp.dot(hidden, down_matrix, preferred_element_type=jnp.float32)
        result = jnp.where(in_range[:, None], result, jnp.float32(0.0))
        return (running.at[chosen].add(result), None)
    summed, _ = lax.scan(one_route, jnp.zeros((TOKENS, D), jnp.float32), jnp.arange(2 * EXPERTS, dtype=jnp.int32))
    return (widened + gating[:, None] * summed).astype(jnp.bfloat16)
```

```python
import functools

import jax
import jax.numpy as jnp
from jax import lax
from jax.experimental import pallas as pl
from jax.experimental.pallas import tpu as pltpu
from jax.sharding import PartitionSpec as P

EXPERTS = 4
CAP = 2
EPSILON = 1e-05
SIDE = 4
NSEM = 224
f32, bf16 = jnp.float32, jnp.bfloat16
MESH = pl.DeviceIdType.MESH


class Sums:
    def __init__(self, send, near, src, q, f, s, q2, f2):
        self.send, self.near = send, near
        self.src, self.q, self.f, self.s, self.q2, self.f2 = src, q, f, s, q2, f2
        self.width = src.shape[3]
        self.part = self.width // 4
        self.m, self.n = {}, {}

    def sel(self, h, k, c, w):
        cols = pl.ds(c, w)
        return self.src.at[:, k, :, cols] if h == 0 else self.src.at[k, :, :, cols]

    def base(self, h):
        return h * 2 * self.part

    def s1(self, h, quarter):
        p, a = self.part, self.base(h)
        plus, minus = self.near(1 - h, 1), self.near(1 - h, -1)
        if quarter == 0:
            self.m[h, 1] = self.send(self.sel(h, 2, a, p), self.q.at[h * 2], plus)
            self.m[h, 4] = self.send(self.sel(h, 3, a, p), self.f.at[h, 1, :, :, pl.ds(0, p)], minus)
        else:
            self.m[h, 2] = self.send(self.sel(h, 2, a + p, p), self.q.at[h * 2 + 1], minus)
            self.m[h, 3] = self.send(self.sel(h, 1, a + p, p), self.f.at[h, 0, :, :, pl.ds(p, p)], plus)

    def s2(self, h, quarter):
        p, a = self.part, self.base(h)
        k, c, which = (1, a, 1) if quarter == 0 else (3, a + p, 2)
        got = self.q.at[h * 2 + quarter]
        self.m[h, which].wait_recv()
        cols = pl.ds(c, p)

        def body(i, _):
            at = (i, k, slice(None), cols) if h == 0 else (k, i, slice(None), cols)
            self.src[at] = (self.src[at].astype(f32) + got[i].astype(f32)).astype(bf16)
            return 0

        lax.fori_loop(0, SIDE, body, 0)
        if quarter == 0:
            self.m[h, 5] = self.send(self.sel(h, 1, c, p), self.f.at[h, 0, :, :, pl.ds(0, p)], self.near(1 - h, 1))
        else:
            self.m[h, 6] = self.send(self.sel(h, 3, c, p), self.f.at[h, 1, :, :, pl.ds(p, p)], self.near(1 - h, -1))

    def s3(self, h):
        for i in (3, 4, 5, 6):
            self.m[h, i].wait_recv()
        p = self.part
        cols = pl.ds(self.base(h), 2 * p)

        def body(i, _):
            at = (i, 0, slice(None), cols) if h == 0 else (0, i, slice(None), cols)
            total = self.src[at].astype(f32) + self.f[h, 0, i].astype(f32) + self.f[h, 1, i].astype(f32)
            self.s[h, i] = total.astype(bf16)
            return 0

        lax.fori_loop(0, SIDE, body, 0)
        plus, minus = self.near(h, 1), self.near(h, -1)
        lo, hi = pl.ds(0, p), pl.ds(p, p)
        self.n[h, 1] = self.send(self.s.at[h, 2, :, lo], self.q2.at[h * 2], plus)
        self.n[h, 2] = self.send(self.s.at[h, 2, :, hi], self.q2.at[h * 2 + 1], minus)
        self.n[h, 3] = self.send(self.s.at[h, 1, :, hi], self.f2.at[h, 0, :, hi], plus)
        self.n[h, 4] = self.send(self.s.at[h, 3, :, lo], self.f2.at[h, 1, :, lo], minus)

    def s5(self, h):
        p = self.part
        lo, hi = pl.ds(0, p), pl.ds(p, p)
        self.n[h, 1].wait_recv()
        self.s[h, 1, :, lo] = (self.s[h, 1, :, lo].astype(f32) + self.q2[h * 2].astype(f32)).astype(bf16)
        self.n[h, 5] = self.send(self.s.at[h, 1, :, lo], self.f2.at[h, 0, :, lo], self.near(h, 1))
        self.n[h, 2].wait_recv()
        self.s[h, 3, :, hi] = (self.s[h, 3, :, hi].astype(f32) + self.q2[h * 2 + 1].astype(f32)).astype(bf16)
        self.n[h, 6] = self.send(self.s.at[h, 3, :, hi], self.f2.at[h, 1, :, hi], self.near(h, -1))

    def s6(self, h):
        for i in (3, 4, 5, 6):
            self.n[h, i].wait_recv()
        return self.s[h, 0].astype(f32) + self.f2[h, 0].astype(f32) + self.f2[h, 1].astype(f32)


class Gather:
    def __init__(self, send, near, dst):
        self.send, self.near, self.dst = send, near, dst
        self.part = dst.shape[3] // 4
        self.m = {}

    def blk(self, h, a, b, c, w):
        i, j = (a, b) if h == 0 else (b, a)
        return self.dst.at[i, j, :, pl.ds(h * 2 * self.part + c, w)]

    def first(self, h, name, a, b, c, w, sign, a2):
        self.m[h, name] = self.send(self.blk(h, a, b, c, w), self.blk(h, a2, b, c, w), self.near(h, sign))

    def second(self, h, name, a, b, c, w, sign, b2):
        self.m[h, name] = self.send(self.blk(h, a, b, c, w), self.blk(h, a, b2, c, w), self.near(1 - h, sign))

    def across(self, h, a):
        p = self.part
        self.second(h, ("p", a), a, 0, 0, 2 * p, 1, 3)
        self.second(h, ("m", a), a, 0, 0, 2 * p, -1, 1)

    def begin(self):
        p = self.part
        for h in (0, 1):
            self.first(h, "p", 0, 0, 0, 2 * p, 1, 3)
            self.first(h, "m", 0, 0, 0, 2 * p, -1, 1)
        for h in (0, 1):
            self.across(h, 0)

    def step1(self, h):
        p = self.part
        self.m[h, "p"].wait_recv()
        self.first(h, "pp", 3, 0, 0, p, 1, 2)
        self.m[h, "m"].wait_recv()
        self.first(h, "mm", 1, 0, p, p, -1, 2)
        self.across(h, 3)
        self.across(h, 1)

    def onward(self, h, a):
        p = self.part
        self.m[h, ("p", a)].wait_recv()
        self.second(h, ("pp", a), a, 3, 0, p, 1, 2)
        self.m[h, ("m", a)].wait_recv()
        self.second(h, ("mm", a), a, 1, p, p, -1, 2)

    def step3(self, h):
        self.m[h, "pp"].wait_recv()
        self.m[h, "mm"].wait_recv()
        self.across(h, 2)

    def end(self):
        for h in (0, 1):
            for a in range(SIDE):
                self.m[h, ("pp", a)].wait_recv()
                self.m[h, ("mm", a)].wait_recv()


def kernel(
    depth, residual, context, out_weight, gain, router, mask, pick, put, unfold, fold, up_hbm, down_hbm, out,
    cg, res, p1, p1q, p1f, p1s, p1q2, p1f2, tiles, heads, resid, folded, outgoing, arrived,
    grid, up, down, acc, hidden, part, rq, rf, rs, rq2, rf2, back, returned, ssem, rsem, wsem,
):
    r, z, t = lax.axis_index("role"), lax.axis_index("exp"), lax.axis_index("tp")
    x, y = t // SIDE, t % SIDE
    width = out.shape[1]
    fold_cols = width // 8
    count = [0]
    sent = []

    def send(src, dst, device):
        k = count[0]
        count[0] += 1
        copy = pltpu.make_async_remote_copy(
            src_ref=src, dst_ref=dst, send_sem=ssem.at[k], recv_sem=rsem.at[k], device_id=device, device_id_type=MESH
        )
        copy.start()
        sent.append(copy)
        return copy

    class Local:
        def __init__(self, src, dst):
            k = count[0]
            count[0] += 1
            self.copy = pltpu.make_async_copy(src, dst, rsem.at[k])
            self.copy.start()

        def wait_recv(self):
            self.copy.wait()

    def near(axis, step):
        if axis == 0:
            return (r, z, lax.rem(x + step + SIDE, SIDE) * SIDE + y)
        return (r, z, x * SIDE + lax.rem(y + step + SIDE, SIDE))

    def peer(dr, dz):
        return (lax.rem(r + dr, 2), lax.rem(z + dz + depth, depth), t)

    loads = [pltpu.make_async_copy(up_hbm, up, wsem.at[0]), pltpu.make_async_copy(down_hbm, down, wsem.at[1])]
    for load in loads:
        load.start()

    barrier = pltpu.get_barrier_semaphore()
    others = [peer(dr, dz) for dz in range(depth) for dr in (0, 1) if (dr, dz) != (0, 0)]
    others += [near(axis, step) for axis in (0, 1) for step in (1, -1)]
    for device in others:
        pl.semaphore_signal(barrier, inc=1, device_id=device, device_id_type=MESH)
    pl.semaphore_wait(barrier, len(others))

    rows = context.shape[0]
    mid = depth // 2
    partner = peer(1, 0)
    up_z, down_z = peer(0, 1), peer(0, -1)
    shared = {0: send(context, cg.at[0, 1], partner)}
    going = send(context, cg.at[depth - 1, 0], up_z)
    coming = send(context, cg.at[1, 0], down_z)

    def project(dz, own):
        shared[dz].wait_recv()
        both = jnp.concatenate([own, cg[dz, 1]], axis=0)
        res[...] = jnp.dot(both, out_weight[...], preferred_element_type=f32)

        def body(i, _):
            dx, dy = i // SIDE, i % SIDE
            home = lax.rem(x + dx, SIDE) * SIDE + lax.rem(y + dy, SIDE)
            at = pl.multiple_of(home * 8, 8)
            block = jnp.concatenate([res[pl.ds(at, 8), :], res[pl.ds(rows + at, 8), :]], axis=0)
            p1[dx, dy, pl.ds(dz * 16, 16), :] = block.astype(bf16)
            return 0

        lax.fori_loop(0, SIDE * SIDE, body, 0)

    half_rows = rows // 2
    pending = [0]
    for step in range(1, mid):
        a, b = depth - step, step
        going.wait_recv()
        if step < mid - 1:
            going_next = send(cg.at[a, 0], cg.at[a - 1, 0], up_z)
        else:
            going_next = send(cg.at[a, 0, pl.ds(0, half_rows)], cg.at[mid, 0, pl.ds(0, half_rows)], up_z)
        shared[a] = send(cg.at[a, 0], cg.at[a, 1], partner)
        coming.wait_recv()
        if step < mid - 1:
            coming_next = send(cg.at[b, 0], cg.at[b + 1, 0], down_z)
        else:
            coming_next = send(cg.at[b, 0, pl.ds(half_rows, half_rows)], cg.at[mid, 0, pl.ds(half_rows, half_rows)], down_z)
        shared[b] = send(cg.at[b, 0], cg.at[b, 1], partner)
        going, coming = going_next, coming_next
        for dz in pending:
            project(dz, context[...] if dz == 0 else cg[dz, 0])
        pending = [a, b]
    going.wait_recv()
    coming.wait_recv()
    shared[mid] = send(cg.at[mid, 0], cg.at[mid, 1], partner)
    for dz in pending + [mid]:
        project(dz, cg[dz, 0])

    heads_sum = Sums(send, near, p1, p1q, p1f, p1s, p1q2, p1f2)
    for quarter in (0, 1):
        for h in (0, 1):
            heads_sum.s1(h, quarter)
    for quarter in (0, 1):
        for h in (0, 1):
            heads_sum.s2(h, quarter)
    for h in (0, 1):
        heads_sum.s3(h)
    for h in (0, 1):
        heads_sum.s5(h)
    final = [heads_sum.s6(h) for h in (0, 1)]
    for i in range(2 * depth):
        tiles[i] = jnp.concatenate([final[0][8 * i : 8 * i + 8], final[1][8 * i : 8 * i + 8]], axis=0).astype(bf16)

    mine = r * depth + z
    columns = []
    for dz in range(depth):
        for dr in (0, 1):
            src, dst = tiles.at[dz * 2 + dr], heads.at[mine]
            columns.append(Local(src, dst) if (dr, dz) == (0, 0) else send(src, dst, peer(dr, dz)))
    for copy in columns:
        copy.wait_recv()
    group = width // (2 * depth)
    squares = jnp.zeros((8, group), f32)
    for g in range(2 * depth):
        block = heads[g].astype(f32)
        whole = jnp.concatenate([block[:8], block[8:]], axis=1)
        cols = slice(g * group, (g + 1) * group)
        value = (residual[:, cols].astype(f32) + whole).astype(bf16).astype(f32)
        resid[:, cols] = value
        squares = squares + value * value
    inverse = lax.rsqrt(jnp.sum(squares, axis=1, keepdims=True) / width + EPSILON)
    logits = jnp.zeros((8, fold_cols), f32)
    choice = mask[...]
    for j in range(0, 8, 2):
        pair = []
        for i in (j, j + 1):
            cols = slice(i * fold_cols, (i + 1) * fold_cols)
            normed = (resid[:, cols] * inverse * gain[:, cols].astype(f32)).astype(bf16).astype(f32)
            rows_of = router[:, cols].astype(f32)
            picked = choice[:, 0:1] * rows_of[0:1]
            for e in range(1, 2 * EXPERTS):
                picked = picked + choice[:, e : e + 1] * rows_of[e : e + 1]
            logits = logits + normed * picked
            pair.append(normed)
        folded[pl.ds(j * 8, 16), :] = jnp.concatenate(pair, axis=0).astype(bf16)
    slots = jnp.dot(pick[...], folded[...], preferred_element_type=f32).astype(bf16)
    outgoing[...] = slots.reshape(outgoing.shape)
    gating = jax.nn.sigmoid(jnp.sum(logits, axis=1, keepdims=True))

    halves = depth // EXPERTS
    dispatched = {}
    for dr in (0, 1):
        for dz in range(depth):
            to = peer(dr, dz)
            src, dst = outgoing.at[to[0] * EXPERTS + to[1] // halves], arrived.at[dr, dz]
            dispatched[dr, dz] = Local(src, dst) if (dr, dz) == (0, 0) else send(src, dst, to)

    gathers = [Gather(send, near, grid.at[w]) for w in (0, 1)]
    sums = [
        Sums(send, near, part.at[w], rq.at[w], rf.at[w], rs.at[w], rq2.at[w], rf2.at[w]) for w in (0, 1)
    ]
    slot_rows = 2 * depth

    def enter(w):
        for dz in range(depth):
            dispatched[w, dz].wait_recv()
        block = arrived[w].reshape(8 * slot_rows, fold_cols)
        lines = jnp.dot(unfold[...], block, preferred_element_type=f32).astype(bf16)
        for j in range(8):
            grid[w, 0, 0, :, pl.ds(j * fold_cols, fold_cols)] = lines[j * slot_rows : (j + 1) * slot_rows]
        gathers[w].begin()

    many = SIDE * SIDE * slot_rows
    chunk = width // 16

    def up_piece(w, piece):
        if piece == 0:
            acc[...] = jnp.zeros_like(acc)

        def body(i, _):
            at = pl.ds(pl.multiple_of(i * chunk, chunk), chunk)
            acc[...] += jnp.dot(
                grid[w, :, :, :, at].reshape(many, chunk), up[at, :], preferred_element_type=f32
            )
            return 0

        lax.fori_loop(piece * 4, piece * 4 + 4, body, 0)
        if piece == 3:
            hidden[...] = jax.nn.gelu(acc[...]).astype(bf16)

    def down_piece(w, quarter):
        def body(i, _):
            at = pl.ds(pl.multiple_of(i * chunk, chunk), chunk)
            got = jnp.dot(hidden[...], down[:, at], preferred_element_type=f32)
            part[w, :, :, :, at] = got.astype(bf16).reshape(SIDE, SIDE, slot_rows, chunk)
            return 0

        lax.fori_loop(quarter * 4, quarter * 4 + 4, body, 0)

    def down_and_send(w):
        for quarter in (0, 1):
            for h in (0, 1):
                down_piece(w, 2 * h + quarter)
                sums[w].s1(h, quarter)

    returns = {}

    def leave(w):
        lines = []
        for h in (0, 1):
            total = sums[w].s6(h)
            lines += [total[:, j * fold_cols : (j + 1) * fold_cols] for j in range(4)]
        block = jnp.concatenate(lines, axis=0).astype(bf16)
        back[w] = (
            jnp.dot(fold[...], block, preferred_element_type=f32).astype(bf16).reshape(depth, slot_rows, fold_cols)
        )
        for dz in range(depth):
            src, dst = back.at[w, dz], returned.at[mine]
            returns[w, dz] = Local(src, dst) if (w, dz) == (0, 0) else send(src, dst, peer(w, -dz))

    g0, g1 = gathers
    enter(0)
    for h in (0, 1):
        g0.step1(h)
    for h in (0, 1):
        g0.onward(h, 0)
    for h in (0, 1):
        g0.step3(h)
    enter(1)
    for a in (3, 1):
        for h in (0, 1):
            g0.onward(h, a)
    for h in (0, 1):
        g1.step1(h)
    for h in (0, 1):
        g0.onward(h, 2)
    for h in (0, 1):
        g1.onward(h, 0)
    g0.end()
    loads[0].wait()
    up_piece(0, 0)
    for h in (0, 1):
        g1.step3(h)
    up_piece(0, 1)
    for h in (0, 1):
        g1.onward(h, 3)
    up_piece(0, 2)
    for h in (0, 1):
        g1.onward(h, 1)
    up_piece(0, 3)
    for h in (0, 1):
        g1.onward(h, 2)
    loads[1].wait()
    down_and_send(0)
    g1.end()
    up_piece(1, 0)
    for h in (0, 1):
        sums[0].s2(h, 0)
    up_piece(1, 1)
    for h in (0, 1):
        sums[0].s2(h, 1)
    up_piece(1, 2)
    up_piece(1, 3)
    for h in (0, 1):
        sums[0].s3(h)
    down_and_send(1)
    for h in (0, 1):
        sums[0].s5(h)
    for quarter in (0, 1):
        for h in (0, 1):
            sums[1].s2(h, quarter)
    leave(0)
    for h in (0, 1):
        sums[1].s3(h)
    for h in (0, 1):
        sums[1].s5(h)
    leave(1)
    for w in (0, 1):
        for dz in range(depth):
            returns[w, dz].wait_recv()
    block = returned[...].reshape(2 * depth * slot_rows, fold_cols)
    experts = jnp.dot(put[...], block, preferred_element_type=f32)
    for j in range(8):
        cols = slice(j * fold_cols, (j + 1) * fold_cols)
        out[:, cols] = (resid[:, cols] + gating * experts[j * 8 : j * 8 + 8]).astype(bf16)
    for copy in sent:
        copy.wait_send()
    assert count[0] <= NSEM


def per_device(
    residual_in, context, out_weight, norm_gain, router, up_weight, down_weight, modality, expert
):
    tok_rows, width = residual_in.shape
    depth = lax.axis_size("exp")
    hidden_units = up_weight.shape[3]
    fold_cols = width // 8
    slot_rows = CAP * depth
    routes = modality * EXPERTS + expert
    kinds = 2 * EXPERTS
    hot = routes[:, None] == jnp.arange(kinds, dtype=jnp.int32)[None, :]
    same = (routes[:, None] == routes[None, :]) & (
        jnp.arange(tok_rows)[:, None] > jnp.arange(tok_rows)[None, :]
    )
    target = routes * CAP + jnp.sum(same.astype(jnp.int32), axis=1)
    placed = (jnp.arange(kinds * CAP, dtype=jnp.int32)[:, None] == target[None, :]).astype(f32)
    eye = jnp.eye(8, dtype=f32)
    by_slot = placed.reshape(kinds, CAP, tok_rows)
    pick = jnp.einsum("mcq,ij->mcijq", by_slot, eye).reshape(kinds * CAP * 8, 8 * tok_rows).astype(bf16)
    halves = depth // EXPERTS
    put = jnp.broadcast_to(
        jnp.einsum("mcq,ij->iqmcj", by_slot, eye)[:, :, :, None],
        (8, tok_rows, kinds, halves, CAP, 8),
    ).reshape(8 * tok_rows, kinds * halves * CAP * 8).astype(bf16)
    n = 8 * slot_rows
    line = jnp.arange(n)
    source = (line % slot_rows) // CAP * (CAP * 8) + (line % CAP) * 8 + line // slot_rows
    unfold = (source[:, None] == line[None, :]).astype(bf16)
    fold = (source[None, :] == line[:, None]).astype(bf16)
    rows, group = context.shape[0], out_weight.shape[1]
    q = width // 4
    g4 = group // 4
    vm = pltpu.VMEM
    scratch = [
        vm((depth, 2, rows, context.shape[1]), bf16),
        vm((2 * rows, group), f32),
        vm((4, 4, rows, group), bf16),
        vm((4, 4, rows, g4), bf16),
        vm((2, 2, 4, rows, 2 * g4), bf16),
        vm((2, 4, rows, 2 * g4), bf16),
        vm((4, rows, g4), bf16),
        vm((2, 2, rows, 2 * g4), bf16),
        vm((2 * depth, 16, group // 2), bf16),
        vm((2 * depth, 16, group // 2), bf16),
        vm((tok_rows, width), f32),
        vm((8 * tok_rows, fold_cols), bf16),
        vm((kinds, CAP * 8, fold_cols), bf16),
        vm((2, depth, CAP * 8, fold_cols), bf16),
        vm((2, 4, 4, slot_rows, width), bf16),
        vm((width, hidden_units), bf16),
        vm((hidden_units, width), bf16),
        vm((16 * slot_rows, hidden_units), f32),
        vm((16 * slot_rows, hidden_units), bf16),
        vm((2, 4, 4, slot_rows, width), bf16),
        vm((2, 4, 4, slot_rows, q), bf16),
        vm((2, 2, 2, 4, slot_rows, 2 * q), bf16),
        vm((2, 2, 4, slot_rows, 2 * q), bf16),
        vm((2, 4, slot_rows, q), bf16),
        vm((2, 2, 2, slot_rows, 2 * q), bf16),
        vm((2, depth, CAP * 8, fold_cols), bf16),
        vm((2 * depth, CAP * 8, fold_cols), bf16),
        pltpu.SemaphoreType.DMA((NSEM,)),
        pltpu.SemaphoreType.DMA((NSEM,)),
        pltpu.SemaphoreType.DMA((2,)),
    ]
    local = pl.BlockSpec(memory_space=pltpu.VMEM)
    there = pl.BlockSpec(memory_space=pl.ANY)
    return pl.pallas_call(
        functools.partial(kernel, depth),
        out_shape=jax.ShapeDtypeStruct((tok_rows, width), bf16),
        in_specs=[local] * 10 + [there] * 2,
        out_specs=local,
        scratch_shapes=scratch,
        compiler_params=pltpu.CompilerParams(
            collective_id=0, has_side_effects=True, vmem_limit_bytes=63_000_000
        ),
    )(
        residual_in,
        context,
        out_weight,
        norm_gain.reshape(1, width),
        router.reshape(kinds, width),
        hot.astype(f32),
        pick,
        put,
        unfold,
        fold,
        up_weight.reshape(width, hidden_units),
        down_weight.reshape(hidden_units, width),
    )


def solution(mesh):
    in_specs = (
        P(("role", "exp", "tp"), None),
        P(("role", "exp"), "tp"),
        P("tp", ("role", "exp")),
        P(),
        P(),
        P("role", "exp", None, "tp"),
        P("role", "exp", "tp", None),
        P(("role", "exp", "tp")),
        P(("role", "exp", "tp")),
    )
    out_specs = P(("role", "exp", "tp"), None)
    return jax.shard_map(
        per_device, mesh=mesh, in_specs=in_specs, out_specs=out_specs, check_vma=False
    )
```

```python
import functools

import jax
import jax.numpy as jnp
from jax import lax
from jax.experimental import pallas as pl
from jax.experimental.pallas import tpu as pltpu
from jax.sharding import PartitionSpec as P

EXPERTS = 4
CAP = 2
EPSILON = 1e-05
SIDE = 4
NSEM = 256
f32, bf16 = jnp.float32, jnp.bfloat16
MESH = pl.DeviceIdType.MESH


class Sums:
    def __init__(self, send, near, src, q, f, s, q2, f2):
        self.send, self.near = send, near
        self.src, self.q, self.f, self.s, self.q2, self.f2 = src, q, f, s, q2, f2
        self.width = src.shape[3]
        self.part = self.width // 4
        self.m, self.n = {}, {}

    def sel(self, h, k, c, w):
        cols = pl.ds(c, w)
        return self.src.at[:, k, :, cols] if h == 0 else self.src.at[k, :, :, cols]

    def base(self, h):
        return h * 2 * self.part

    def s1(self, h, quarter):
        p, a = self.part, self.base(h)
        plus, minus = self.near(1 - h, 1), self.near(1 - h, -1)
        if quarter == 0:
            self.m[h, 1] = self.send(self.sel(h, 2, a, p), self.q.at[h * 2], plus)
            self.m[h, 4] = self.send(self.sel(h, 3, a, p), self.f.at[h, 1, :, :, pl.ds(0, p)], minus)
        else:
            self.m[h, 2] = self.send(self.sel(h, 2, a + p, p), self.q.at[h * 2 + 1], minus)
            self.m[h, 3] = self.send(self.sel(h, 1, a + p, p), self.f.at[h, 0, :, :, pl.ds(p, p)], plus)

    def s2(self, h, quarter):
        p, a = self.part, self.base(h)
        k, c, which = (1, a, 1) if quarter == 0 else (3, a + p, 2)
        got = self.q.at[h * 2 + quarter]
        self.m[h, which].wait_recv()
        cols = pl.ds(c, p)

        def body(i, _):
            at = (i, k, slice(None), cols) if h == 0 else (k, i, slice(None), cols)
            self.src[at] = (self.src[at].astype(f32) + got[i].astype(f32)).astype(bf16)
            return 0

        lax.fori_loop(0, SIDE, body, 0)
        if quarter == 0:
            self.m[h, 5] = self.send(self.sel(h, 1, c, p), self.f.at[h, 0, :, :, pl.ds(0, p)], self.near(1 - h, 1))
        else:
            self.m[h, 6] = self.send(self.sel(h, 3, c, p), self.f.at[h, 1, :, :, pl.ds(p, p)], self.near(1 - h, -1))

    def s3(self, h):
        for i in (3, 4, 5, 6):
            self.m[h, i].wait_recv()
        p = self.part
        cols = pl.ds(self.base(h), 2 * p)

        def body(i, _):
            at = (i, 0, slice(None), cols) if h == 0 else (0, i, slice(None), cols)
            total = self.src[at].astype(f32) + self.f[h, 0, i].astype(f32) + self.f[h, 1, i].astype(f32)
            self.s[h, i] = total.astype(bf16)
            return 0

        lax.fori_loop(0, SIDE, body, 0)
        plus, minus = self.near(h, 1), self.near(h, -1)
        lo, hi = pl.ds(0, p), pl.ds(p, p)
        self.n[h, 1] = self.send(self.s.at[h, 2, :, lo], self.q2.at[h * 2], plus)
        self.n[h, 2] = self.send(self.s.at[h, 2, :, hi], self.q2.at[h * 2 + 1], minus)
        self.n[h, 3] = self.send(self.s.at[h, 1, :, hi], self.f2.at[h, 0, :, hi], plus)
        self.n[h, 4] = self.send(self.s.at[h, 3, :, lo], self.f2.at[h, 1, :, lo], minus)

    def s5(self, h):
        p = self.part
        lo, hi = pl.ds(0, p), pl.ds(p, p)
        self.n[h, 1].wait_recv()
        self.s[h, 1, :, lo] = (self.s[h, 1, :, lo].astype(f32) + self.q2[h * 2].astype(f32)).astype(bf16)
        self.n[h, 5] = self.send(self.s.at[h, 1, :, lo], self.f2.at[h, 0, :, lo], self.near(h, 1))
        self.n[h, 2].wait_recv()
        self.s[h, 3, :, hi] = (self.s[h, 3, :, hi].astype(f32) + self.q2[h * 2 + 1].astype(f32)).astype(bf16)
        self.n[h, 6] = self.send(self.s.at[h, 3, :, hi], self.f2.at[h, 1, :, hi], self.near(h, -1))

    def s6(self, h):
        for i in (3, 4, 5, 6):
            self.n[h, i].wait_recv()
        return self.s[h, 0].astype(f32) + self.f2[h, 0].astype(f32) + self.f2[h, 1].astype(f32)


class Gather:
    def __init__(self, send, near, dst):
        self.send, self.near, self.dst = send, near, dst
        self.part = dst.shape[3] // 4
        self.m = {}

    def blk(self, h, a, b, c, w):
        i, j = (a, b) if h == 0 else (b, a)
        return self.dst.at[i, j, :, pl.ds(h * 2 * self.part + c, w)]

    def first(self, h, name, a, b, c, w, sign, a2):
        self.m[h, name] = self.send(self.blk(h, a, b, c, w), self.blk(h, a2, b, c, w), self.near(h, sign))

    def second(self, h, name, a, b, c, w, sign, b2):
        self.m[h, name] = self.send(self.blk(h, a, b, c, w), self.blk(h, a, b2, c, w), self.near(1 - h, sign))

    def across(self, h, a):
        p = self.part
        self.second(h, ("p", a), a, 0, 0, 2 * p, 1, 3)
        self.second(h, ("m", a), a, 0, 0, 2 * p, -1, 1)

    def begin(self):
        p = self.part
        for h in (0, 1):
            self.first(h, "p", 0, 0, 0, 2 * p, 1, 3)
            self.first(h, "m", 0, 0, 0, 2 * p, -1, 1)
        for h in (0, 1):
            self.across(h, 0)

    def step1(self, h):
        p = self.part
        self.m[h, "p"].wait_recv()
        self.first(h, "pp", 3, 0, 0, p, 1, 2)
        self.m[h, "m"].wait_recv()
        self.first(h, "mm", 1, 0, p, p, -1, 2)
        self.across(h, 3)
        self.across(h, 1)

    def onward(self, h, a):
        p = self.part
        self.m[h, ("p", a)].wait_recv()
        self.second(h, ("pp", a), a, 3, 0, p, 1, 2)
        self.m[h, ("m", a)].wait_recv()
        self.second(h, ("mm", a), a, 1, p, p, -1, 2)

    def step3(self, h):
        self.m[h, "pp"].wait_recv()
        self.m[h, "mm"].wait_recv()
        self.across(h, 2)

    def end(self):
        for h in (0, 1):
            for a in range(SIDE):
                self.m[h, ("pp", a)].wait_recv()
                self.m[h, ("mm", a)].wait_recv()


def kernel(
    depth, modality, expert, residual_in, context, out_weight_in, gain_in, router_in, up_hbm, down_hbm, out,
    residual, out_weight, gain, router, pick, put, unfold, fold, cg, res, wave_a, wave_b, tiles, heads, resid, folded,
    outgoing, arrived, grid, up, down, acc, hidden, part, rq, rf, rs, rq2, rf2, back, returned, ssem, rsem, wsem,
):
    r, z, t = lax.axis_index("role"), lax.axis_index("exp"), lax.axis_index("tp")
    x, y = t // SIDE, t % SIDE
    width = out.shape[1]
    fold_cols = width // 8
    count = [0]
    sent = []

    def send(src, dst, device):
        k = count[0]
        count[0] += 1
        copy = pltpu.make_async_remote_copy(
            src_ref=src, dst_ref=dst, send_sem=ssem.at[k], recv_sem=rsem.at[k], device_id=device, device_id_type=MESH
        )
        copy.start()
        sent.append(copy)
        return copy

    class Local:
        def __init__(self, src, dst):
            k = count[0]
            count[0] += 1
            self.copy = pltpu.make_async_copy(src, dst, rsem.at[k])
            self.copy.start()

        def wait_recv(self):
            self.copy.wait()

    def near(axis, step):
        if axis == 0:
            return (r, z, lax.rem(x + step + SIDE, SIDE) * SIDE + y)
        return (r, z, x * SIDE + lax.rem(y + step + SIDE, SIDE))

    def peer(dr, dz):
        return (lax.rem(r + dr, 2), lax.rem(z + dz + depth, depth), t)

    mid = depth // 2
    barrier = pltpu.get_barrier_semaphore()
    others = [peer(dr, dz) for dz in range(depth) for dr in (0, 1) if (dr, dz) != (0, 0)]
    others += [near(axis, step) for axis in (0, 1) for step in (1, -1)]
    for device in others:
        pl.semaphore_signal(barrier, inc=1, device_id=device, device_id_type=MESH)
    pairs = [(context, cg.at[0, 0]), (out_weight_in, out_weight), (residual_in, residual), (gain_in, gain),
             (router_in, router), (up_hbm, up), (down_hbm, down)]
    loads = [pltpu.make_async_copy(src, dst, wsem.at[i]) for i, (src, dst) in enumerate(pairs)]
    for load in loads:
        load.start()

    routes = [modality[i] * EXPERTS + expert[i] for i in range(8)]
    slot_of = []
    for i in range(8):
        place = routes[i] * CAP
        for k in range(i):
            place = place + jnp.where(routes[k] == routes[i], 1, 0)
        slot_of.append(place)

    def spread(values, index):
        total = jnp.zeros(index.shape, jnp.int32)
        for i, value in enumerate(values):
            total = jnp.where(index == i, value, total)
        return total

    def table(shape):
        return (lax.broadcasted_iota(jnp.int32, shape, 0), lax.broadcasted_iota(jnp.int32, shape, 1))

    row, col = table(pick.shape)
    pick[...] = jnp.where(((row >> 3) == spread(slot_of, col & 7)) & ((row & 7) == (col >> 3)), 1.0, 0.0).astype(bf16)
    row, col = table(put.shape)
    slot = (col >> 5) * 2 + ((col >> 3) & 1)
    put[...] = jnp.where((slot == spread(slot_of, row & 7)) & ((col & 7) == (row >> 3)), 1.0, 0.0).astype(bf16)
    row, col = table(unfold.shape)
    unfold[...] = jnp.where(((row & 15) >> 1) * 16 + (row & 1) * 8 + (row >> 4) == col, 1.0, 0.0).astype(bf16)
    fold[...] = jnp.where(((col & 15) >> 1) * 16 + (col & 1) * 8 + (col >> 4) == row, 1.0, 0.0).astype(bf16)
    row, col = table((8, 1))
    route_rows = spread(routes, row)
    loads[0].wait()
    pl.semaphore_wait(barrier, len(others))

    rows = cg.shape[2]
    half_rows = rows // 2
    partner, up_z, down_z = peer(1, 0), peer(0, 1), peer(0, -1)
    piece = [pl.ds(0, half_rows), pl.ds(half_rows, half_rows)]

    def pass_on(a, b, c, device):
        return send(cg.at[a, 0, piece[c]], cg.at[b, 0, piece[c]], device)

    def hand_over(a, c):
        return send(cg.at[a, 0, piece[c]], cg.at[a, 1, piece[c]], partner)

    going = {0: pass_on(0, depth - 1, 0, up_z)}
    coming = {0: pass_on(0, 1, 0, down_z)}
    shared = {0: [send(cg.at[0, 0], cg.at[0, 1], partner)]}
    going[1] = pass_on(0, depth - 1, 1, up_z)
    coming[1] = pass_on(0, 1, 1, down_z)
    loads[1].wait()

    order = [0, 1, depth - 1, 2, depth - 2, 3, depth - 3, mid]
    first = 5

    def project(dz):
        for copy in shared[dz]:
            copy.wait_recv()
        at_wave = order.index(dz)
        p1, low = (wave_a[0], at_wave * 16) if at_wave < first else (wave_b[0], (at_wave - first) * 16)
        both = jnp.concatenate([cg[dz, 0], cg[dz, 1]], axis=0)
        res[...] = jnp.dot(both, out_weight[...], preferred_element_type=f32)

        def body(i, _):
            dx, dy = i // SIDE, i % SIDE
            home = lax.rem(x + dx, SIDE) * SIDE + lax.rem(y + dy, SIDE)
            at = pl.multiple_of(home * 8, 8)
            block = jnp.concatenate([res[pl.ds(at, 8), :], res[pl.ds(rows + at, 8), :]], axis=0)
            p1[dx, dy, pl.ds(low, 16), :] = block.astype(bf16)
            return 0

        lax.fori_loop(0, SIDE * SIDE, body, 0)

    def ring_step(step):
        nonlocal going, coming
        a, b = depth - step, step
        shared[a], shared[b] = [], []
        going_next, coming_next = {}, {}
        for c in (0, 1):
            going[c].wait_recv()
            if step < mid - 1 or c == 0:
                going_next[c] = pass_on(a, a - 1, c, up_z)
            coming[c].wait_recv()
            if step < mid - 1 or c == 1:
                coming_next[c] = pass_on(b, b + 1, c, down_z)
            shared[a].append(hand_over(a, c))
            shared[b].append(hand_over(b, c))
        going, coming = going_next, coming_next

    sum_a, sum_b = Sums(send, near, *wave_a), Sums(send, near, *wave_b)
    both_halves = (0, 1)

    def each(step, *rest):
        for args in rest or ((),):
            for h in both_halves:
                step(h, *args)

    ring_step(1)
    project(0)
    ring_step(2)
    project(depth - 1)
    project(1)
    ring_step(3)
    project(depth - 2)
    project(2)
    each(sum_a.s1, (0,), (1,))
    going[0].wait_recv()
    shared[mid] = [hand_over(mid, 0)]
    coming[1].wait_recv()
    shared[mid].append(hand_over(mid, 1))
    project(depth - 3)
    project(3)
    each(sum_a.s2, (0,))
    project(mid)
    each(sum_b.s1, (0,), (1,))
    each(sum_a.s2, (1,))
    each(sum_a.s3)
    each(sum_b.s2, (0,), (1,))
    each(sum_a.s5)
    each(sum_b.s3)
    mine = r * depth + z
    columns = {}

    def to_tokens(total, dzs):
        final = [total.s6(h) for h in both_halves]
        for i, dz in enumerate(dzs):
            for dr in (0, 1):
                at = slice(i * 16 + dr * 8, i * 16 + dr * 8 + 8)
                tiles[dz * 2 + dr] = jnp.concatenate([final[0][at], final[1][at]], axis=0).astype(bf16)
        for dz in dzs:
            for dr in (0, 1):
                src, dst = tiles.at[dz * 2 + dr], heads.at[mine]
                columns[dr, dz] = Local(src, dst) if (dr, dz) == (0, 0) else send(src, dst, peer(dr, dz))

    to_tokens(sum_a, order[:first])
    each(sum_b.s5)
    to_tokens(sum_b, order[first:])
    for load in loads[2:5]:
        load.wait()

    group = width // (2 * depth)
    squares = jnp.zeros((8, group), f32)
    for dz in order:
        for dr in (0, 1):
            columns[dr, dz].wait_recv()
            source = lax.rem(r + dr, 2) * depth + lax.rem(z - dz + depth, depth)
            block = heads[source].astype(f32)
            whole = jnp.concatenate([block[:8], block[8:]], axis=1)
            cols = pl.ds(pl.multiple_of(source * group, group), group)
            value = (residual[:, cols].astype(f32) + whole).astype(bf16).astype(f32)
            resid[:, cols] = value
            squares = squares + value * value
    inverse = lax.rsqrt(jnp.sum(squares, axis=1, keepdims=True) / width + EPSILON)
    logits = jnp.zeros((8, fold_cols), f32)
    lanes = gain.shape[1]
    per_fold = fold_cols // lanes
    for j in range(0, 8, 2):
        pair = []
        for i in (j, j + 1):
            cols = slice(i * fold_cols, (i + 1) * fold_cols)
            gains = gain[pl.ds(i * per_fold, per_fold), :].astype(f32)
            gains = jnp.concatenate(
                [jnp.broadcast_to(gains[k : k + 1], (8, lanes)) for k in range(per_fold)], axis=1
            )
            normed = (resid[:, cols] * inverse * gains).astype(bf16).astype(f32)
            picked = jnp.zeros((8, fold_cols), f32)
            for e in range(2 * EXPERTS):
                line = router[e // EXPERTS, :, cols].astype(f32)[e % EXPERTS : e % EXPERTS + 1]
                picked = jnp.where(route_rows == e, line, picked)
            logits = logits + normed * picked
            pair.append(normed)
        folded[pl.ds(j * 8, 16), :] = jnp.concatenate(pair, axis=0).astype(bf16)
    slots = jnp.dot(pick[...], folded[...], preferred_element_type=f32).astype(bf16)
    outgoing[...] = slots.reshape(outgoing.shape)
    gating = jax.nn.sigmoid(jnp.sum(logits, axis=1, keepdims=True))

    halves = depth // EXPERTS
    dispatched = {}
    for dr in (0, 1):
        for dz in range(depth):
            to = peer(dr, dz)
            src, dst = outgoing.at[to[0] * EXPERTS + to[1] // halves], arrived.at[dr, dz]
            dispatched[dr, dz] = Local(src, dst) if (dr, dz) == (0, 0) else send(src, dst, to)

    gathers = [Gather(send, near, grid.at[w]) for w in (0, 1)]
    sums = [
        Sums(send, near, part.at[w], rq.at[w], rf.at[w], rs.at[w], rq2.at[w], rf2.at[w]) for w in (0, 1)
    ]
    slot_rows = 2 * depth

    def enter(w):
        for dz in range(depth):
            dispatched[w, dz].wait_recv()
        block = arrived[w].reshape(8 * slot_rows, fold_cols)
        lines = jnp.dot(unfold[...], block, preferred_element_type=f32).astype(bf16)
        for j in range(8):
            grid[w, 0, 0, :, pl.ds(j * fold_cols, fold_cols)] = lines[j * slot_rows : (j + 1) * slot_rows]
        gathers[w].begin()

    many = SIDE * SIDE * slot_rows
    chunk = width // 16

    def up_piece(w, piece):
        if piece == 0:
            acc[...] = jnp.zeros_like(acc)

        def body(i, _):
            at = pl.ds(pl.multiple_of(i * chunk, chunk), chunk)
            acc[...] += jnp.dot(
                grid[w, :, :, :, at].reshape(many, chunk), up[at, :], preferred_element_type=f32
            )
            return 0

        lax.fori_loop(piece * 4, piece * 4 + 4, body, 0)
        if piece == 3:
            hidden[...] = jax.nn.gelu(acc[...]).astype(bf16)

    def down_piece(w, quarter):
        def body(i, _):
            at = pl.ds(pl.multiple_of(i * chunk, chunk), chunk)
            got = jnp.dot(hidden[...], down[:, at], preferred_element_type=f32)
            part[w, :, :, :, at] = got.astype(bf16).reshape(SIDE, SIDE, slot_rows, chunk)
            return 0

        lax.fori_loop(quarter * 4, quarter * 4 + 4, body, 0)

    def down_and_send(w):
        for quarter in (0, 1):
            for h in (0, 1):
                down_piece(w, 2 * h + quarter)
                sums[w].s1(h, quarter)

    returns = {}

    def leave(w):
        lines = []
        for h in (0, 1):
            total = sums[w].s6(h)
            lines += [total[:, j * fold_cols : (j + 1) * fold_cols] for j in range(4)]
        block = jnp.concatenate(lines, axis=0).astype(bf16)
        back[w] = (
            jnp.dot(fold[...], block, preferred_element_type=f32).astype(bf16).reshape(depth, slot_rows, fold_cols)
        )
        for dz in range(depth):
            src, dst = back.at[w, dz], returned.at[mine]
            returns[w, dz] = Local(src, dst) if (w, dz) == (0, 0) else send(src, dst, peer(w, -dz))

    g0, g1 = gathers
    enter(0)
    for h in (0, 1):
        g0.step1(h)
    for h in (0, 1):
        g0.onward(h, 0)
    for h in (0, 1):
        g0.step3(h)
    enter(1)
    for a in (3, 1):
        for h in (0, 1):
            g0.onward(h, a)
    for h in (0, 1):
        g1.step1(h)
    for h in (0, 1):
        g0.onward(h, 2)
    for h in (0, 1):
        g1.onward(h, 0)
    g0.end()
    loads[5].wait()
    up_piece(0, 0)
    for h in (0, 1):
        g1.step3(h)
    up_piece(0, 1)
    for h in (0, 1):
        g1.onward(h, 3)
    up_piece(0, 2)
    for h in (0, 1):
        g1.onward(h, 1)
    up_piece(0, 3)
    for h in (0, 1):
        g1.onward(h, 2)
    loads[6].wait()
    down_and_send(0)
    g1.end()
    up_piece(1, 0)
    for h in (0, 1):
        sums[0].s2(h, 0)
    up_piece(1, 1)
    for h in (0, 1):
        sums[0].s2(h, 1)
    up_piece(1, 2)
    up_piece(1, 3)
    for h in (0, 1):
        sums[0].s3(h)
    down_and_send(1)
    for h in (0, 1):
        sums[0].s5(h)
    for quarter in (0, 1):
        for h in (0, 1):
            sums[1].s2(h, quarter)
    leave(0)
    for h in (0, 1):
        sums[1].s3(h)
    for h in (0, 1):
        sums[1].s5(h)
    leave(1)
    for w in (0, 1):
        for dz in range(depth):
            returns[w, dz].wait_recv()
    block = returned[...].reshape(2 * depth * slot_rows, fold_cols)
    experts = jnp.dot(put[...], block, preferred_element_type=f32)
    for j in range(8):
        cols = slice(j * fold_cols, (j + 1) * fold_cols)
        out[:, cols] = (resid[:, cols] + gating * experts[j * 8 : j * 8 + 8]).astype(bf16)
    for copy in sent:
        copy.wait_send()
    assert count[0] <= NSEM


def per_device(
    residual_in, context, out_weight, norm_gain, router, up_weight, down_weight, modality, expert
):
    tok_rows, width = residual_in.shape
    depth = lax.axis_size("exp")
    hidden_units = up_weight.shape[3]
    fold_cols = width // 8
    slot_rows = CAP * depth
    kinds = 2 * EXPERTS
    rows, group = context.shape[0], out_weight.shape[1]
    q = width // 4
    g4 = group // 4
    vm = pltpu.VMEM

    def sum_buffers(lines):
        return [
            vm((4, 4, lines, group), bf16),
            vm((4, 4, lines, g4), bf16),
            vm((2, 2, 4, lines, 2 * g4), bf16),
            vm((2, 4, lines, 2 * g4), bf16),
            vm((4, lines, g4), bf16),
            vm((2, 2, lines, 2 * g4), bf16),
        ]

    scratch = [
        vm((tok_rows, width), bf16),
        vm(out_weight.shape, bf16),
        vm((width // 128, 128), bf16),
        vm(router.shape, bf16),
        vm((kinds * CAP * 8, 8 * tok_rows), bf16),
        vm((8 * tok_rows, 2 * depth * CAP * 8), bf16),
        vm((8 * slot_rows, 8 * slot_rows), bf16),
        vm((8 * slot_rows, 8 * slot_rows), bf16),
        vm((depth, 2, rows, context.shape[1]), bf16),
        vm((2 * rows, group), f32),
        sum_buffers(80),
        sum_buffers(48),
        vm((2 * depth, 16, group // 2), bf16),
        vm((2 * depth, 16, group // 2), bf16),
        vm((tok_rows, width), f32),
        vm((8 * tok_rows, fold_cols), bf16),
        vm((kinds, CAP * 8, fold_cols), bf16),
        vm((2, depth, CAP * 8, fold_cols), bf16),
        vm((2, 4, 4, slot_rows, width), bf16),
        vm((width, hidden_units), bf16),
        vm((hidden_units, width), bf16),
        vm((16 * slot_rows, hidden_units), f32),
        vm((16 * slot_rows, hidden_units), bf16),
        vm((2, 4, 4, slot_rows, width), bf16),
        vm((2, 4, 4, slot_rows, q), bf16),
        vm((2, 2, 2, 4, slot_rows, 2 * q), bf16),
        vm((2, 2, 4, slot_rows, 2 * q), bf16),
        vm((2, 4, slot_rows, q), bf16),
        vm((2, 2, 2, slot_rows, 2 * q), bf16),
        vm((2, depth, CAP * 8, fold_cols), bf16),
        vm((2 * depth, CAP * 8, fold_cols), bf16),
        pltpu.SemaphoreType.DMA((NSEM,)),
        pltpu.SemaphoreType.DMA((NSEM,)),
        pltpu.SemaphoreType.DMA((7,)),
    ]
    local = pl.BlockSpec(memory_space=pltpu.VMEM)
    there = pl.BlockSpec(memory_space=pl.ANY)
    return pl.pallas_call(
        functools.partial(kernel, depth),
        out_shape=jax.ShapeDtypeStruct((tok_rows, width), bf16),
        in_specs=[pl.BlockSpec(memory_space=pltpu.SMEM)] * 2 + [there] * 7,
        out_specs=local,
        scratch_shapes=scratch,
        compiler_params=pltpu.CompilerParams(
            collective_id=0, has_side_effects=True, vmem_limit_bytes=63_000_000
        ),
    )(
        modality,
        expert,
        residual_in,
        context,
        out_weight,
        norm_gain.reshape(width // 128, 128),
        router,
        up_weight.reshape(width, hidden_units),
        down_weight.reshape(hidden_units, width),
    )


def solution(mesh):
    in_specs = (
        P(("role", "exp", "tp"), None),
        P(("role", "exp"), "tp"),
        P("tp", ("role", "exp")),
        P(),
        P(),
        P("role", "exp", None, "tp"),
        P("role", "exp", "tp", None),
        P(("role", "exp", "tp")),
        P(("role", "exp", "tp")),
    )
    out_specs = P(("role", "exp", "tp"), None)
    return jax.shard_map(
        per_device, mesh=mesh, in_specs=in_specs, out_specs=out_specs, check_vma=False
    )
```

```python
import functools

import jax
import jax.numpy as jnp
from jax import lax
from jax.experimental import pallas as pl
from jax.experimental.pallas import tpu as pltpu
from jax.sharding import PartitionSpec as P

EXPERTS = 4
CAP = 2
EPSILON = 1e-05
SIDE = 4
NSEM = 320
f32, bf16 = jnp.float32, jnp.bfloat16
MESH = pl.DeviceIdType.MESH


class Sums:
    def __init__(self, send, near, src, q, f, s, q2, f2, side=None, arrivals=None):
        self.send, self.near, self.side, self.arrivals = send, near, side, arrivals
        self.src, self.q, self.f, self.s, self.q2, self.f2 = src, q, f, s, q2, f2
        self.m, self.n = {}, {}

    def sel(self, h, k, quarter):
        at = 2 * h + quarter
        return self.src.at[at, :, k] if h == 0 else self.src.at[at, k]

    def add_side(self, h, quarter, *ks):
        if self.side is None or (h, quarter) != (0, 0):
            return
        cols = pl.ds(0, self.side.shape[3])
        for k in ks:
            self.arrivals[k].wait_recv()

            def body(i, _, k=k):
                was = self.src[0, i, k, :, cols].astype(f32)
                self.src[0, i, k, :, cols] = (was + self.side[k, i].astype(f32)).astype(bf16)
                return 0

            lax.fori_loop(0, SIDE, body, 0)

    def s1(self, h, quarter):
        self.add_side(h, quarter, 2, 3)
        plus, minus = self.near(1 - h, 1), self.near(1 - h, -1)
        if quarter == 0:
            self.m[h, 1] = self.send(self.sel(h, 2, 0), self.q.at[h * 2], plus)
            self.m[h, 4] = self.send(self.sel(h, 3, 0), self.f.at[h, 1, 0], minus)
        else:
            self.m[h, 2] = self.send(self.sel(h, 2, 1), self.q.at[h * 2 + 1], minus)
            self.m[h, 3] = self.send(self.sel(h, 1, 1), self.f.at[h, 0, 1], plus)

    def s2(self, h, quarter):
        k, which = (1, 1) if quarter == 0 else (3, 2)
        at = 2 * h + quarter
        got = self.q.at[at]
        self.add_side(h, quarter, 1)
        self.m[h, which].wait_recv()

        def body(i, _):
            where = (at, i, k) if h == 0 else (at, k, i)
            self.src[where] = (self.src[where].astype(f32) + got[i].astype(f32)).astype(bf16)
            return 0

        lax.fori_loop(0, SIDE, body, 0)
        if quarter == 0:
            self.m[h, 5] = self.send(self.sel(h, 1, 0), self.f.at[h, 0, 0], self.near(1 - h, 1))
        else:
            self.m[h, 6] = self.send(self.sel(h, 3, 1), self.f.at[h, 1, 1], self.near(1 - h, -1))

    def s3(self, h):
        self.add_side(h, 0, 0)
        for i in (3, 4, 5, 6):
            self.m[h, i].wait_recv()

        def body(i, _):
            for quarter in (0, 1):
                at = 2 * h + quarter
                where = (at, i, 0) if h == 0 else (at, 0, i)
                total = self.src[where].astype(f32) + self.f[h, 0, quarter, i].astype(f32)
                self.s[h, quarter, i] = (total + self.f[h, 1, quarter, i].astype(f32)).astype(bf16)
            return 0

        lax.fori_loop(0, SIDE, body, 0)
        plus, minus = self.near(h, 1), self.near(h, -1)
        self.n[h, 1] = self.send(self.s.at[h, 0, 2], self.q2.at[h * 2], plus)
        self.n[h, 2] = self.send(self.s.at[h, 1, 2], self.q2.at[h * 2 + 1], minus)
        self.n[h, 3] = self.send(self.s.at[h, 1, 1], self.f2.at[h, 0, 1], plus)
        self.n[h, 4] = self.send(self.s.at[h, 0, 3], self.f2.at[h, 1, 0], minus)

    def s5(self, h):
        self.n[h, 1].wait_recv()
        self.s[h, 0, 1] = (self.s[h, 0, 1].astype(f32) + self.q2[h * 2].astype(f32)).astype(bf16)
        self.n[h, 5] = self.send(self.s.at[h, 0, 1], self.f2.at[h, 0, 0], self.near(h, 1))
        self.n[h, 2].wait_recv()
        self.s[h, 1, 3] = (self.s[h, 1, 3].astype(f32) + self.q2[h * 2 + 1].astype(f32)).astype(bf16)
        self.n[h, 6] = self.send(self.s.at[h, 1, 3], self.f2.at[h, 1, 1], self.near(h, -1))

    def s6(self, h):
        for i in (3, 4, 5, 6):
            self.n[h, i].wait_recv()
        parts = []
        for quarter in (0, 1):
            total = self.s[h, quarter, 0].astype(f32) + self.f2[h, 0, quarter].astype(f32)
            parts.append(total + self.f2[h, 1, quarter].astype(f32))
        return jnp.concatenate(parts, axis=1)


class Gather:
    def __init__(self, send, near, dst, base, twin):
        self.send, self.near, self.dst, self.base, self.twin = send, near, dst, base, twin
        self.part = (dst.shape[3] - base) // 4
        self.m = {}

    def blk(self, h, a, b, c, w):
        i, j = (a, b) if h == 0 else (b, a)
        return self.dst.at[i, j, :, pl.ds(self.base + h * 2 * self.part + c, w)]

    def first(self, h, name, a, b, c, w, sign, a2):
        self.m[h, name] = self.send(self.blk(h, a, b, c, w), self.blk(h, a2, b, c, w), self.near(h, sign))

    def second(self, h, name, a, b, c, w, sign, b2):
        self.m[h, name] = self.send(self.blk(h, a, b, c, w), self.blk(h, a, b2, c, w), self.near(1 - h, sign))

    def over(self, h, a, b):
        if h == 0:
            near, far = self.dst.at[a, b, :, pl.ds(self.base, self.base)], self.dst.at[a, b, :, pl.ds(0, self.base)]
            self.m["z", a, b] = self.send(near, far, self.twin)

    def across(self, h, a):
        p = self.part
        self.second(h, ("p", a), a, 0, 0, 2 * p, 1, 3)
        self.second(h, ("m", a), a, 0, 0, 2 * p, -1, 1)

    def begin(self):
        p = self.part
        for h in (0, 1):
            self.first(h, "p", 0, 0, 0, 2 * p, 1, 3)
            self.first(h, "m", 0, 0, 0, 2 * p, -1, 1)
        for h in (0, 1):
            self.across(h, 0)

    def step1(self, h):
        p = self.part
        self.m[h, "p"].wait_recv()
        self.first(h, "pp", 3, 0, 0, p, 1, 2)
        self.m[h, "m"].wait_recv()
        self.first(h, "mm", 1, 0, p, p, -1, 2)
        self.across(h, 3)
        self.across(h, 1)
        self.over(h, 3, 0)
        self.over(h, 1, 0)

    def onward(self, h, a):
        p = self.part
        self.m[h, ("p", a)].wait_recv()
        self.second(h, ("pp", a), a, 3, 0, p, 1, 2)
        self.m[h, ("m", a)].wait_recv()
        self.second(h, ("mm", a), a, 1, p, p, -1, 2)
        self.over(h, a, 3)
        self.over(h, a, 1)

    def step3(self, h):
        self.m[h, "pp"].wait_recv()
        self.m[h, "mm"].wait_recv()
        self.across(h, 2)
        self.over(h, 2, 0)

    def last(self, a):
        for h in (0, 1):
            self.m[h, ("pp", a)].wait_recv()
            self.m[h, ("mm", a)].wait_recv()
            self.over(h, a, 2)

    def end(self):
        for a in range(SIDE):
            for b in range(SIDE):
                if (a, b) != (0, 0):
                    self.m["z", a, b].wait_recv()


def kernel(
    depth, modality, expert, residual_in, context, out_weight_in, gain_in, router_in, up_hbm, down_hbm, out,
    residual, out_weight, gain, router, pick, put, unfold, fold, cg, res, wave_bufs, tiles, heads, resid, folded,
    outgoing, arrived, grid, up, down, acc, hidden, part, side_out, side_in, rq, rf, rs, rq2, rf2, back, returned, ssem, rsem, wsem,
):
    r, z, t = lax.axis_index("role"), lax.axis_index("exp"), lax.axis_index("tp")
    x, y = t // SIDE, t % SIDE
    width = out.shape[1]
    fold_cols = width // 8
    count = [0]
    sent = []

    def send(src, dst, device):
        k = count[0]
        count[0] += 1
        copy = pltpu.make_async_remote_copy(
            src_ref=src, dst_ref=dst, send_sem=ssem.at[k], recv_sem=rsem.at[k], device_id=device, device_id_type=MESH
        )
        copy.start()
        sent.append(copy)
        return copy

    class Local:
        def __init__(self, src, dst):
            k = count[0]
            count[0] += 1
            self.copy = pltpu.make_async_copy(src, dst, rsem.at[k])
            self.copy.start()

        def wait_recv(self):
            self.copy.wait()

    def near(axis, step):
        if axis == 0:
            return (r, z, lax.rem(x + step + SIDE, SIDE) * SIDE + y)
        return (r, z, x * SIDE + lax.rem(y + step + SIDE, SIDE))

    def peer(dr, dz):
        return (lax.rem(r + dr, 2), lax.rem(z + dz + depth, depth), t)

    mid = depth // 2
    parity = lax.rem(z, 2)
    twin = (r, z + 1 - 2 * parity, t)
    barrier = pltpu.get_barrier_semaphore()
    others = [peer(dr, dz) for dz in range(depth) for dr in (0, 1) if (dr, dz) != (0, 0)]
    others += [near(axis, step) for axis in (0, 1) for step in (1, -1)]
    for device in others:
        pl.semaphore_signal(barrier, inc=1, device_id=device, device_id_type=MESH)
    pairs = [(context, cg.at[0, 0]), (out_weight_in, out_weight), (residual_in, residual), (gain_in, gain),
             (router_in, router)]
    for k, at in enumerate([parity, 1 - parity]):
        here, there = pl.ds(k * fold_cols, fold_cols), pl.ds(pl.multiple_of(at * fold_cols, fold_cols), fold_cols)
        pairs += [(up_hbm.at[there], up.at[here]), (down_hbm.at[:, there], down.at[:, here])]
    rest = pl.ds(2 * fold_cols, width - 2 * fold_cols)
    pairs += [(up_hbm.at[rest], up.at[rest]), (down_hbm.at[:, rest], down.at[:, rest])]
    loads = [pltpu.make_async_copy(src, dst, wsem.at[i]) for i, (src, dst) in enumerate(pairs)]
    for load in loads:
        load.start()

    routes = [modality[i] * EXPERTS + expert[i] for i in range(8)]
    slot_of = []
    for i in range(8):
        place = routes[i] * CAP
        for k in range(i):
            place = place + jnp.where(routes[k] == routes[i], 1, 0)
        slot_of.append(place)

    def spread(values, index):
        total = jnp.zeros(index.shape, jnp.int32)
        for i, value in enumerate(values):
            total = jnp.where(index == i, value, total)
        return total

    def table(shape):
        return (lax.broadcasted_iota(jnp.int32, shape, 0), lax.broadcasted_iota(jnp.int32, shape, 1))

    row, col = table(pick.shape)
    pick[...] = jnp.where(((row >> 3) == spread(slot_of, col & 7)) & ((row & 7) == (col >> 3)), 1.0, 0.0).astype(bf16)
    row, col = table(put.shape)
    slot = (col >> 5) * 2 + ((col >> 3) & 1)
    put[...] = jnp.where((slot == spread(slot_of, row & 7)) & ((col & 7) == (row >> 3)), 1.0, 0.0).astype(bf16)
    row, col = table(unfold.shape)
    unfold[...] = jnp.where(((row & 15) >> 1) * 16 + (row & 1) * 8 + (row >> 4) == col, 1.0, 0.0).astype(bf16)
    fold[...] = jnp.where(((col & 15) >> 1) * 16 + (col & 1) * 8 + (col >> 4) == row, 1.0, 0.0).astype(bf16)
    row, col = table((8, 1))
    route_rows = spread(routes, row)
    loads[0].wait()
    pl.semaphore_wait(barrier, len(others))

    rows = cg.shape[2]
    half_rows = rows // 2
    partner, up_z, down_z = peer(1, 0), peer(0, 1), peer(0, -1)
    piece = [pl.ds(0, half_rows), pl.ds(half_rows, half_rows)]

    def pass_on(a, b, c, device):
        return send(cg.at[a, 0, piece[c]], cg.at[b, 0, piece[c]], device)

    def hand_over(a, c):
        return send(cg.at[a, 0, piece[c]], cg.at[a, 1, piece[c]], partner)

    going = {0: pass_on(0, depth - 1, 0, up_z)}
    coming = {0: pass_on(0, 1, 0, down_z)}
    shared = {0: [send(cg.at[0, 0], cg.at[0, 1], partner)]}
    going[1] = pass_on(0, depth - 1, 1, up_z)
    coming[1] = pass_on(0, 1, 1, down_z)
    loads[1].wait()

    wide = out_weight.shape[1] // 4
    waves = [[0, 1, depth - 1], [2, depth - 2], [3, depth - 3, mid]]
    order = [dz for wave in waves for dz in wave]

    def project(dz):
        for copy in shared[dz]:
            copy.wait_recv()
        k = [dz in wave for wave in waves].index(True)
        p1, low = wave_bufs[k][0], waves[k].index(dz) * 16
        both = jnp.concatenate([cg[dz, 0], cg[dz, 1]], axis=0)
        res[...] = jnp.dot(both, out_weight[...], preferred_element_type=f32)

        def body(i, _):
            dx, dy = i // SIDE, i % SIDE
            home = lax.rem(x + dx, SIDE) * SIDE + lax.rem(y + dy, SIDE)
            at = pl.multiple_of(home * 8, 8)
            block = jnp.concatenate([res[pl.ds(at, 8), :], res[pl.ds(rows + at, 8), :]], axis=0)
            for quarter in range(4):
                cols = slice(quarter * wide, (quarter + 1) * wide)
                p1[quarter, dx, dy, pl.ds(low, 16), :] = block[:, cols].astype(bf16)
            return 0

        lax.fori_loop(0, SIDE * SIDE, body, 0)

    def ring_step(step):
        nonlocal going, coming
        a, b = depth - step, step
        shared[a], shared[b] = [], []
        going_next, coming_next = {}, {}
        for c in (0, 1):
            going[c].wait_recv()
            if step < mid - 1 or c == 0:
                going_next[c] = pass_on(a, a - 1, c, up_z)
            coming[c].wait_recv()
            if step < mid - 1 or c == 1:
                coming_next[c] = pass_on(b, b + 1, c, down_z)
            shared[a].append(hand_over(a, c))
            shared[b].append(hand_over(b, c))
        going, coming = going_next, coming_next

    early = [Sums(send, near, *buffers) for buffers in wave_bufs]
    both_halves = (0, 1)

    def each(step, *rest):
        for args in rest or ((),):
            for h in both_halves:
                step(h, *args)

    mine = r * depth + z
    columns = {}

    def to_tokens(k):
        final = [early[k].s6(h) for h in both_halves]
        for i, dz in enumerate(waves[k]):
            for dr in (0, 1):
                at = slice(i * 16 + dr * 8, i * 16 + dr * 8 + 8)
                tiles[dz * 2 + dr] = jnp.concatenate([final[0][at], final[1][at]], axis=0).astype(bf16)
        for dz in waves[k]:
            for dr in (0, 1):
                src, dst = tiles.at[dz * 2 + dr], heads.at[mine]
                columns[dr, dz] = Local(src, dst) if (dr, dz) == (0, 0) else send(src, dst, peer(dr, dz))

    w0, w1, w2 = early
    ring_step(1)
    project(0)
    project(depth - 1)
    project(1)
    each(w0.s1, (0,), (1,))
    ring_step(2)
    project(depth - 2)
    project(2)
    each(w1.s1, (0,), (1,))
    each(w0.s2, (0,), (1,))
    ring_step(3)
    project(depth - 3)
    project(3)
    each(w0.s3)
    going[0].wait_recv()
    shared[mid] = [hand_over(mid, 0)]
    coming[1].wait_recv()
    shared[mid].append(hand_over(mid, 1))
    each(w1.s2, (0,), (1,))
    project(mid)
    each(w2.s1, (0,), (1,))
    each(w0.s5)
    each(w1.s3)
    each(w2.s2, (0,), (1,))
    to_tokens(0)
    each(w1.s5)
    each(w2.s3)
    to_tokens(1)
    each(w2.s5)
    to_tokens(2)
    for load in loads[2:5]:
        load.wait()

    group = width // (2 * depth)
    squares = jnp.zeros((8, group), f32)
    for dz in order:
        for dr in (0, 1):
            columns[dr, dz].wait_recv()
            source = lax.rem(r + dr, 2) * depth + lax.rem(z - dz + depth, depth)
            block = heads[source].astype(f32)
            whole = jnp.concatenate([block[:8], block[8:]], axis=1)
            cols = pl.ds(pl.multiple_of(source * group, group), group)
            value = (residual[:, cols].astype(f32) + whole).astype(bf16).astype(f32)
            resid[:, cols] = value
            squares = squares + value * value
    inverse = lax.rsqrt(jnp.sum(squares, axis=1, keepdims=True) / width + EPSILON)
    logits = jnp.zeros((8, fold_cols), f32)
    lanes = gain.shape[1]
    per_fold = fold_cols // lanes
    for j in range(0, 8, 2):
        pair = []
        for i in (j, j + 1):
            cols = slice(i * fold_cols, (i + 1) * fold_cols)
            gains = gain[pl.ds(i * per_fold, per_fold), :].astype(f32)
            gains = jnp.concatenate(
                [jnp.broadcast_to(gains[k : k + 1], (8, lanes)) for k in range(per_fold)], axis=1
            )
            normed = (resid[:, cols] * inverse * gains).astype(bf16).astype(f32)
            picked = jnp.zeros((8, fold_cols), f32)
            for e in range(2 * EXPERTS):
                line = router[e // EXPERTS, :, cols].astype(f32)[e % EXPERTS : e % EXPERTS + 1]
                picked = jnp.where(route_rows == e, line, picked)
            logits = logits + normed * picked
            pair.append(normed)
        folded[pl.ds(j * 8, 16), :] = jnp.concatenate(pair, axis=0).astype(bf16)
    slots = jnp.dot(pick[...], folded[...], preferred_element_type=f32).astype(bf16)
    outgoing[...] = slots.reshape(outgoing.shape)
    gating = jax.nn.sigmoid(jnp.sum(logits, axis=1, keepdims=True))

    halves = depth // EXPERTS
    dispatched = {}
    for dr in (0, 1):
        for dz in range(depth):
            to = peer(dr, dz)
            src, dst = outgoing.at[to[0] * EXPERTS + to[1] // halves], arrived.at[dr, z]
            dispatched[dr, dz] = Local(src, dst) if (dr, dz) == (0, 0) else send(src, dst, to)

    side_sent = [{}, {}]
    gathers = [Gather(send, near, grid.at[w], fold_cols, twin) for w in (0, 1)]
    sums = [
        Sums(send, near, part.at[w], rq.at[w], rf.at[w], rs.at[w], rq2.at[w], rf2.at[w], side_in.at[w], side_sent[w])
        for w in (0, 1)
    ]
    slot_rows = 2 * depth

    def enter(w):
        for dz in range(depth):
            dispatched[w, dz].wait_recv()
        block = arrived[w].reshape(8 * slot_rows, fold_cols)
        lines = jnp.dot(unfold[...], block, preferred_element_type=f32).astype(bf16)
        for j in range(8):
            at = lax.rem(parity + j, 2) if j < 2 else j
            cols = pl.ds(pl.multiple_of(at * fold_cols, fold_cols), fold_cols)
            grid[w, 0, 0, :, cols] = lines[j * slot_rows : (j + 1) * slot_rows]
        gathers[w].begin()

    many = SIDE * SIDE * slot_rows
    chunk = width // 16

    def up_piece(w, piece):
        if piece == 0:
            acc[...] = jnp.zeros_like(acc)

        def body(i, _):
            at = pl.ds(pl.multiple_of(i * chunk, chunk), chunk)
            acc[...] += jnp.dot(
                grid[w, :, :, :, at].reshape(many, chunk), up[at, :], preferred_element_type=f32
            )
            return 0

        lax.fori_loop(piece * 4, piece * 4 + 4, body, 0)
        if piece == 3:
            hidden[...] = jax.nn.gelu(acc[...]).astype(bf16)

    def down_side(w):
        side_chunk = fold_cols // 2

        def body(i, _):
            at = pl.ds(pl.multiple_of(i * side_chunk, side_chunk), side_chunk)
            got = jnp.dot(hidden[...], down[:, at], preferred_element_type=f32)
            got = got.astype(bf16).reshape(SIDE, SIDE, slot_rows, side_chunk)
            for k in range(SIDE):
                side_out[w, k, :, :, at] = got[:, k]
            return 0

        lax.fori_loop(0, 2, body, 0)
        for k in (2, 3, 1, 0):
            side_sent[w][k] = send(side_out.at[w, k], side_in.at[w, k], twin)

    out_part = (width - fold_cols) // 4
    out_chunk = out_part // 7

    def down_piece(w, quarter):
        def body(i, _):
            here = pl.ds(pl.multiple_of(i * out_chunk, out_chunk), out_chunk)
            at = pl.ds(pl.multiple_of(fold_cols + (quarter * 7 + i) * out_chunk, out_chunk), out_chunk)
            got = jnp.dot(hidden[...], down[:, at], preferred_element_type=f32)
            part[w, quarter, :, :, :, here] = got.astype(bf16).reshape(SIDE, SIDE, slot_rows, out_chunk)
            return 0

        lax.fori_loop(0, 7, body, 0)

    def down_and_send(w):
        down_side(w)
        for h, quarter in ((1, 0), (0, 1), (1, 1), (0, 0)):
            down_piece(w, 2 * h + quarter)
            sums[w].s1(h, quarter)

    returns = {}

    def leave(w):
        total = jnp.concatenate([sums[w].s6(h) for h in (0, 1)], axis=1)
        mine_too = total[:, :fold_cols]
        lines = [jnp.where(parity == k, 0.0, mine_too) for k in (0, 1)]
        lines += [total[:, j * fold_cols : (j + 1) * fold_cols] for j in range(1, 7)]
        block = jnp.concatenate(lines, axis=0).astype(bf16)
        back[w] = (
            jnp.dot(fold[...], block, preferred_element_type=f32).astype(bf16).reshape(depth, slot_rows, fold_cols)
        )
        for dz in range(depth):
            src, dst = back.at[w, lax.rem(z - dz + depth, depth)], returned.at[mine]
            returns[w, dz] = Local(src, dst) if (w, dz) == (0, 0) else send(src, dst, peer(w, -dz))

    g0, g1 = gathers
    enter(0)
    each(g0.step1)
    each(g0.onward, (0,))
    each(g0.step3)
    enter(1)
    each(g0.onward, (3,), (1,))
    g0.last(0)
    each(g1.step1)
    each(g0.onward, (2,))
    g0.last(3)
    g0.last(1)
    each(g1.onward, (0,))
    g0.last(2)
    g0.end()
    for i in (5, 7, 9):
        loads[i].wait()
    up_piece(0, 0)
    each(g1.step3)
    up_piece(0, 1)
    each(g1.onward, (3,))
    up_piece(0, 2)
    each(g1.onward, (1,))
    g1.last(0)
    up_piece(0, 3)
    each(g1.onward, (2,))
    g1.last(3)
    g1.last(1)
    for i in (6, 8, 10):
        loads[i].wait()
    down_and_send(0)
    g1.last(2)
    g1.end()
    up_piece(1, 0)
    each(sums[0].s2, (0,))
    up_piece(1, 1)
    each(sums[0].s2, (1,))
    up_piece(1, 2)
    up_piece(1, 3)
    each(sums[0].s3)
    down_and_send(1)
    each(sums[0].s5)
    each(sums[1].s2, (0,), (1,))
    leave(0)
    each(sums[1].s3)
    each(sums[1].s5)
    leave(1)
    for w in (0, 1):
        for dz in range(depth):
            returns[w, dz].wait_recv()
    block = returned[...].reshape(2 * depth * slot_rows, fold_cols)
    experts = jnp.dot(put[...], block, preferred_element_type=f32)
    for j in range(8):
        cols = slice(j * fold_cols, (j + 1) * fold_cols)
        out[:, cols] = (resid[:, cols] + gating * experts[j * 8 : j * 8 + 8]).astype(bf16)
    for copy in sent:
        copy.wait_send()
    assert count[0] <= NSEM


def per_device(
    residual_in, context, out_weight, norm_gain, router, up_weight, down_weight, modality, expert
):
    tok_rows, width = residual_in.shape
    depth = lax.axis_size("exp")
    hidden_units = up_weight.shape[3]
    fold_cols = width // 8
    slot_rows = CAP * depth
    kinds = 2 * EXPERTS
    rows, group = context.shape[0], out_weight.shape[1]
    q = (width - fold_cols) // 4
    g4 = group // 4
    vm = pltpu.VMEM

    def sum_buffers(lines):
        return [
            vm((4, 4, 4, lines, g4), bf16),
            vm((4, 4, lines, g4), bf16),
            vm((2, 2, 2, 4, lines, g4), bf16),
            vm((2, 2, 4, lines, g4), bf16),
            vm((4, lines, g4), bf16),
            vm((2, 2, 2, lines, g4), bf16),
        ]

    scratch = [
        vm((tok_rows, width), bf16),
        vm(out_weight.shape, bf16),
        vm((width // 128, 128), bf16),
        vm(router.shape, bf16),
        vm((kinds * CAP * 8, 8 * tok_rows), bf16),
        vm((8 * tok_rows, 2 * depth * CAP * 8), bf16),
        vm((8 * slot_rows, 8 * slot_rows), bf16),
        vm((8 * slot_rows, 8 * slot_rows), bf16),
        vm((depth, 2, rows, context.shape[1]), bf16),
        vm((2 * rows, group), f32),
        [sum_buffers(48), sum_buffers(32), sum_buffers(48)],
        vm((2 * depth, 16, group // 2), bf16),
        vm((2 * depth, 16, group // 2), bf16),
        vm((tok_rows, width), f32),
        vm((8 * tok_rows, fold_cols), bf16),
        vm((kinds, CAP * 8, fold_cols), bf16),
        vm((2, depth, CAP * 8, fold_cols), bf16),
        vm((2, 4, 4, slot_rows, width), bf16),
        vm((width, hidden_units), bf16),
        vm((hidden_units, width), bf16),
        vm((16 * slot_rows, hidden_units), f32),
        vm((16 * slot_rows, hidden_units), bf16),
        vm((2, 4, 4, 4, slot_rows, q), bf16),
        vm((2, 4, 4, slot_rows, fold_cols), bf16),
        vm((2, 4, 4, slot_rows, fold_cols), bf16),
        vm((2, 4, 4, slot_rows, q), bf16),
        vm((2, 2, 2, 2, 4, slot_rows, q), bf16),
        vm((2, 2, 2, 4, slot_rows, q), bf16),
        vm((2, 4, slot_rows, q), bf16),
        vm((2, 2, 2, 2, slot_rows, q), bf16),
        vm((2, depth, CAP * 8, fold_cols), bf16),
        vm((2 * depth, CAP * 8, fold_cols), bf16),
        pltpu.SemaphoreType.DMA((NSEM,)),
        pltpu.SemaphoreType.DMA((NSEM,)),
        pltpu.SemaphoreType.DMA((11,)),
    ]
    local = pl.BlockSpec(memory_space=pltpu.VMEM)
    there = pl.BlockSpec(memory_space=pl.ANY)
    return pl.pallas_call(
        functools.partial(kernel, depth),
        out_shape=jax.ShapeDtypeStruct((tok_rows, width), bf16),
        in_specs=[pl.BlockSpec(memory_space=pltpu.SMEM)] * 2 + [there] * 7,
        out_specs=local,
        scratch_shapes=scratch,
        compiler_params=pltpu.CompilerParams(
            collective_id=0, has_side_effects=True, vmem_limit_bytes=63_000_000
        ),
    )(
        modality,
        expert,
        residual_in,
        context,
        out_weight,
        norm_gain.reshape(width // 128, 128),
        router,
        up_weight.reshape(width, hidden_units),
        down_weight.reshape(hidden_units, width),
    )


def solution(mesh):
    in_specs = (
        P(("role", "exp", "tp"), None),
        P(("role", "exp"), "tp"),
        P("tp", ("role", "exp")),
        P(),
        P(),
        P("role", "exp", None, "tp"),
        P("role", "exp", "tp", None),
        P(("role", "exp", "tp")),
        P(("role", "exp", "tp")),
    )
    out_specs = P(("role", "exp", "tp"), None)
    return jax.shard_map(
        per_device, mesh=mesh, in_specs=in_specs, out_specs=out_specs, check_vma=False
    )
```

```python
import functools

import jax
import jax.numpy as jnp
from jax import lax
from jax.experimental import pallas as pl
from jax.experimental.pallas import tpu as pltpu
from jax.sharding import PartitionSpec as P

EXPERTS = 4
CAP = 2
EPSILON = 1e-05
SIDE = 4
NSEM = 496
f32, bf16 = jnp.float32, jnp.bfloat16
MESH = pl.DeviceIdType.MESH


class Sums:
    def __init__(self, send, near, src, q, f, s, q2, f2, side=None, arrivals=None):
        self.send, self.near, self.side, self.arrivals = send, near, side, arrivals
        self.src, self.q, self.f, self.s, self.q2, self.f2 = src, q, f, s, q2, f2
        self.m, self.n = {}, {}

    def sel(self, h, k, quarter):
        at = 2 * h + quarter
        return self.src.at[at, :, k] if h == 0 else self.src.at[at, k]

    def add_side(self, h, quarter, *ks):
        if self.side is None or (h, quarter) != (0, 0):
            return
        cols = pl.ds(0, self.side.shape[3])
        for k in ks:
            self.arrivals[k].wait_recv()

            def body(i, _, k=k):
                was = self.src[0, i, k, :, cols].astype(f32)
                self.src[0, i, k, :, cols] = (was + self.side[k, i].astype(f32)).astype(bf16)
                return 0

            lax.fori_loop(0, SIDE, body, 0)

    def s1(self, h, quarter):
        self.add_side(h, quarter, 2, 3)
        plus, minus = self.near(1 - h, 1), self.near(1 - h, -1)
        if quarter == 0:
            self.m[h, 1] = self.send(self.sel(h, 2, 0), self.q.at[h * 2], plus)
            self.m[h, 4] = self.send(self.sel(h, 3, 0), self.f.at[h, 1, 0], minus)
        else:
            self.m[h, 2] = self.send(self.sel(h, 2, 1), self.q.at[h * 2 + 1], minus)
            self.m[h, 3] = self.send(self.sel(h, 1, 1), self.f.at[h, 0, 1], plus)

    def s2(self, h, quarter):
        k, which = (1, 1) if quarter == 0 else (3, 2)
        at = 2 * h + quarter
        got = self.q.at[at]
        self.add_side(h, quarter, 1)
        self.m[h, which].wait_recv()

        def body(i, _):
            where = (at, i, k) if h == 0 else (at, k, i)
            self.src[where] = (self.src[where].astype(f32) + got[i].astype(f32)).astype(bf16)
            return 0

        lax.fori_loop(0, SIDE, body, 0)
        if quarter == 0:
            self.m[h, 5] = self.send(self.sel(h, 1, 0), self.f.at[h, 0, 0], self.near(1 - h, 1))
        else:
            self.m[h, 6] = self.send(self.sel(h, 3, 1), self.f.at[h, 1, 1], self.near(1 - h, -1))

    def s3(self, h):
        self.add_side(h, 0, 0)
        for i in (3, 4, 5, 6):
            self.m[h, i].wait_recv()

        def body(i, _):
            for quarter in (0, 1):
                at = 2 * h + quarter
                where = (at, i, 0) if h == 0 else (at, 0, i)
                total = self.src[where].astype(f32) + self.f[h, 0, quarter, i].astype(f32)
                self.s[h, quarter, i] = (total + self.f[h, 1, quarter, i].astype(f32)).astype(bf16)
            return 0

        lax.fori_loop(0, SIDE, body, 0)
        plus, minus = self.near(h, 1), self.near(h, -1)
        self.n[h, 1] = self.send(self.s.at[h, 0, 2], self.q2.at[h * 2], plus)
        self.n[h, 2] = self.send(self.s.at[h, 1, 2], self.q2.at[h * 2 + 1], minus)
        self.n[h, 3] = self.send(self.s.at[h, 1, 1], self.f2.at[h, 0, 1], plus)
        self.n[h, 4] = self.send(self.s.at[h, 0, 3], self.f2.at[h, 1, 0], minus)

    def s5(self, h):
        self.n[h, 1].wait_recv()
        self.s[h, 0, 1] = (self.s[h, 0, 1].astype(f32) + self.q2[h * 2].astype(f32)).astype(bf16)
        self.n[h, 5] = self.send(self.s.at[h, 0, 1], self.f2.at[h, 0, 0], self.near(h, 1))
        self.n[h, 2].wait_recv()
        self.s[h, 1, 3] = (self.s[h, 1, 3].astype(f32) + self.q2[h * 2 + 1].astype(f32)).astype(bf16)
        self.n[h, 6] = self.send(self.s.at[h, 1, 3], self.f2.at[h, 1, 1], self.near(h, -1))

    def s6(self, h):
        for i in (3, 4, 5, 6):
            self.n[h, i].wait_recv()
        parts = []
        for quarter in (0, 1):
            total = self.s[h, quarter, 0].astype(f32) + self.f2[h, 0, quarter].astype(f32)
            parts.append(total + self.f2[h, 1, quarter].astype(f32))
        return jnp.concatenate(parts, axis=1)


class Gather:
    def __init__(self, send, near, dst, base, twin):
        self.send, self.near, self.dst, self.base, self.twin = send, near, dst, base, twin
        self.part = (dst.shape[3] - base) // 4
        self.m = {}

    def blk(self, h, a, b, c, w):
        i, j = (a, b) if h == 0 else (b, a)
        return self.dst.at[i, j, :, pl.ds(self.base + h * 2 * self.part + c, w)]

    def first(self, h, name, a, b, c, w, sign, a2):
        self.m[h, name] = self.send(self.blk(h, a, b, c, w), self.blk(h, a2, b, c, w), self.near(h, sign))

    def second(self, h, name, a, b, c, w, sign, b2):
        self.m[h, name] = self.send(self.blk(h, a, b, c, w), self.blk(h, a, b2, c, w), self.near(1 - h, sign))

    def over(self, h, a, b):
        if h == 0:
            near, far = self.dst.at[a, b, :, pl.ds(self.base, self.base)], self.dst.at[a, b, :, pl.ds(0, self.base)]
            self.m["z", a, b] = self.send(near, far, self.twin)

    def across(self, h, a):
        p = self.part
        self.second(h, ("p", a), a, 0, 0, 2 * p, 1, 3)
        self.second(h, ("m", a), a, 0, 0, 2 * p, -1, 1)

    def begin(self):
        p = self.part
        for h in (0, 1):
            self.first(h, "p", 0, 0, 0, 2 * p, 1, 3)
            self.first(h, "m", 0, 0, 0, 2 * p, -1, 1)
        for h in (0, 1):
            self.across(h, 0)

    def step1(self, h):
        p = self.part
        self.m[h, "p"].wait_recv()
        self.first(h, "pp", 3, 0, 0, p, 1, 2)
        self.m[h, "m"].wait_recv()
        self.first(h, "mm", 1, 0, p, p, -1, 2)
        self.across(h, 3)
        self.across(h, 1)
        self.over(h, 3, 0)
        self.over(h, 1, 0)

    def onward(self, h, a):
        p = self.part
        self.m[h, ("p", a)].wait_recv()
        self.second(h, ("pp", a), a, 3, 0, p, 1, 2)
        self.m[h, ("m", a)].wait_recv()
        self.second(h, ("mm", a), a, 1, p, p, -1, 2)
        self.over(h, a, 3)
        self.over(h, a, 1)

    def step3(self, h):
        self.m[h, "pp"].wait_recv()
        self.m[h, "mm"].wait_recv()
        self.across(h, 2)
        self.over(h, 2, 0)

    def last(self, a):
        for h in (0, 1):
            self.m[h, ("pp", a)].wait_recv()
            self.m[h, ("mm", a)].wait_recv()
            self.over(h, a, 2)

    def end(self):
        for a in range(SIDE):
            for b in range(SIDE):
                if (a, b) != (0, 0):
                    self.m["z", a, b].wait_recv()


def kernel(
    depth, modality, expert, residual_in, context, out_weight_in, gain_in, router_in, up_hbm, down_hbm, out,
    residual, out_weight, gain, router, put, fold, fold_small, tags, tags_in, residual_cols, cg, res, wave_bufs, stack, tiles, heads,
    resid, outgoing, arrived, grid, up, down, acc, hidden, part, back, returned, ssem, rsem, wsem,
):
    r, z, t = lax.axis_index("role"), lax.axis_index("exp"), lax.axis_index("tp")
    x, y = t // SIDE, t % SIDE
    width = out.shape[1]
    fold_cols = width // 8
    count = [0]
    sent = []

    def send(src, dst, device, landed=None):
        k = count[0]
        count[0] += 1
        copy = pltpu.make_async_remote_copy(
            src_ref=src,
            dst_ref=dst,
            send_sem=ssem.at[k],
            recv_sem=rsem.at[k] if landed is None else landed,
            device_id=device,
            device_id_type=MESH,
        )
        copy.start()
        sent.append(copy)
        return copy

    class Local:
        def __init__(self, src, dst):
            k = count[0]
            count[0] += 1
            self.copy = pltpu.make_async_copy(src, dst, rsem.at[k])
            self.copy.start()

        def wait_recv(self):
            self.copy.wait()

    def near(axis, step):
        if axis == 0:
            return (r, z, lax.rem(x + step + SIDE, SIDE) * SIDE + y)
        return (r, z, x * SIDE + lax.rem(y + step + SIDE, SIDE))

    def peer(dr, dz):
        return (lax.rem(r + dr, 2), lax.rem(z + dz + depth, depth), t)

    mid = depth // 2
    parity = lax.rem(z, 2)
    twin = (r, z + 1 - 2 * parity, t)
    barrier = pltpu.get_barrier_semaphore()
    others = [peer(dr, dz) for dz in range(depth) for dr in (0, 1) if (dr, dz) != (0, 0)]
    others += [near(axis, step) for axis in (0, 1) for step in (1, -1)]
    for device in others:
        pl.semaphore_signal(barrier, inc=1, device_id=device, device_id_type=MESH)
    pairs = [(context, cg.at[0, 0]), (out_weight_in, out_weight), (residual_in, residual), (gain_in, gain),
             (router_in, router)]
    for k, at in enumerate([parity, 1 - parity]):
        here, there = pl.ds(k * fold_cols, fold_cols), pl.ds(pl.multiple_of(at * fold_cols, fold_cols), fold_cols)
        pairs += [(up_hbm.at[there], up.at[here]), (down_hbm.at[:, there], down.at[:, here])]
    rest = pl.ds(2 * fold_cols, width - 2 * fold_cols)
    pairs += [(up_hbm.at[rest], up.at[rest]), (down_hbm.at[:, rest], down.at[:, rest])]
    loads = [pltpu.make_async_copy(src, dst, wsem.at[i]) for i, (src, dst) in enumerate(pairs)]
    for load in loads:
        load.start()

    routes = [modality[i] * EXPERTS + expert[i] for i in range(8)]
    slot_of = []
    for i in range(8):
        place = routes[i] * CAP
        for k in range(i):
            place = place + jnp.where(routes[k] == routes[i], 1, 0)
        slot_of.append(place)

    def spread(values, index):
        total = jnp.zeros(index.shape, jnp.int32)
        for i, value in enumerate(values):
            total = jnp.where(index == i, value, total)
        return total

    def table(shape):
        return (lax.broadcasted_iota(jnp.int32, shape, 0), lax.broadcasted_iota(jnp.int32, shape, 1))

    row, col = table(put.shape)
    slot = (col >> 5) * 2 + ((col >> 3) & 1)
    put[...] = jnp.where((slot == spread(slot_of, row & 7)) & ((col & 7) == (row >> 3)), 1.0, 0.0).astype(bf16)
    row, col = table(fold.shape)
    fold[...] = jnp.where(((col & 15) >> 1) * 16 + (col & 1) * 8 + (col >> 4) == row, 1.0, 0.0).astype(bf16)
    row, col = table(fold_small.shape)
    fold_small[...] = jnp.where(((col & 7) >> 1) * 16 + (col & 1) * 8 + (col >> 3) == row, 1.0, 0.0).astype(bf16)
    row, col = table((8, 1))
    route_rows = spread(routes, row)
    tags[...] = spread(slot_of, table(tags.shape)[1] & 7).astype(f32)
    loads[0].wait()
    pl.semaphore_wait(barrier, len(others))

    rows = cg.shape[2]
    half_rows = rows // 2
    partner, up_z, down_z = peer(1, 0), peer(0, 1), peer(0, -1)
    piece = [pl.ds(0, half_rows), pl.ds(half_rows, half_rows)]

    def pass_on(a, b, c, device):
        return send(cg.at[a, 0, piece[c]], cg.at[b, 0, piece[c]], device)

    def hand_over(a, c):
        return send(cg.at[a, 0, piece[c]], cg.at[a, 1, piece[c]], partner)

    going = {0: pass_on(0, depth - 1, 0, up_z)}
    coming = {0: pass_on(0, 1, 0, down_z)}
    shared = {0: [send(cg.at[0, 0], cg.at[0, 1], partner)]}
    going[1] = pass_on(0, depth - 1, 1, up_z)
    coming[1] = pass_on(0, 1, 1, down_z)
    loads[1].wait()

    wide = out_weight.shape[1] // 4
    waves = [[0, 1, depth - 1], [2, depth - 2], [3, depth - 3, mid]]
    order = [dz for wave in waves for dz in wave]

    def project(dz):
        for copy in shared[dz]:
            copy.wait_recv()
        k = [dz in wave for wave in waves].index(True)
        p1, low = wave_bufs[k][0], waves[k].index(dz) * 16
        both = jnp.concatenate([cg[dz, 0], cg[dz, 1]], axis=0)
        res[...] = jnp.dot(both, out_weight[...], preferred_element_type=f32)

        def body(i, _):
            dx, dy = i // SIDE, i % SIDE
            home = lax.rem(x + dx, SIDE) * SIDE + lax.rem(y + dy, SIDE)
            at = pl.multiple_of(home * 8, 8)
            block = jnp.concatenate([res[pl.ds(at, 8), :], res[pl.ds(rows + at, 8), :]], axis=0)
            for quarter in range(4):
                cols = slice(quarter * wide, (quarter + 1) * wide)
                p1[quarter, dx, dy, pl.ds(low, 16), :] = block[:, cols].astype(bf16)
            return 0

        lax.fori_loop(0, SIDE * SIDE, body, 0)

    def ring_step(step):
        nonlocal going, coming
        a, b = depth - step, step
        shared[a], shared[b] = [], []
        going_next, coming_next = {}, {}
        for c in (0, 1):
            going[c].wait_recv()
            if step < mid - 1 or c == 0:
                going_next[c] = pass_on(a, a - 1, c, up_z)
            coming[c].wait_recv()
            if step < mid - 1 or c == 1:
                coming_next[c] = pass_on(b, b + 1, c, down_z)
            shared[a].append(hand_over(a, c))
            shared[b].append(hand_over(b, c))
        going, coming = going_next, coming_next

    early = [Sums(send, near, *buffers) for buffers in wave_bufs]
    both_halves = (0, 1)

    def each(step, *rest):
        for args in rest or ((),):
            for h in both_halves:
                step(h, *args)

    mine = r * depth + z
    columns, extras = {}, {}
    group = width // (2 * depth)

    def to_tokens(k):
        final = [early[k].s6(h) for h in both_halves]
        for i, dz in enumerate(waves[k]):
            pair = []
            for dr in (0, 1):
                at = slice(i * 16 + dr * 8, i * 16 + dr * 8 + 8)
                if dz == 0 and dr == 0:
                    cols = pl.ds(pl.multiple_of(mine * group, group), group)
                    own = residual[:, cols].astype(f32)
                else:
                    extras[dr, -dz % depth][1].wait_recv()
                    own = residual_cols[dr, -dz % depth].astype(f32)
                value = (own + jnp.concatenate([final[0][at], final[1][at]], axis=1)).astype(bf16)
                tiles[dz * 2 + dr] = value
                pair.append(value.astype(f32))
            stack[pl.ds(dz * 16, 16), :] = jnp.concatenate(pair, axis=0).astype(bf16)

    def resid_to_tokens():
        for dz in range(depth):
            for dr in (0, 1):
                src, dst = tiles.at[dz * 2 + dr], heads.at[mine]
                columns[dr, dz] = Local(src, dst) if (dr, dz) == (0, 0) else send(src, dst, peer(dr, dz))

    w0, w1, w2 = early
    ring_step(1)
    project(0)
    project(depth - 1)
    project(1)
    each(w0.s1, (0,), (1,))
    ring_step(2)
    project(depth - 2)
    project(2)
    each(w1.s1, (0,), (1,))
    each(w0.s2, (0,), (1,))
    ring_step(3)
    project(depth - 3)
    project(3)
    each(w0.s3)
    going[0].wait_recv()
    shared[mid] = [hand_over(mid, 0)]
    coming[1].wait_recv()
    shared[mid].append(hand_over(mid, 1))
    each(w1.s2, (0,), (1,))
    loads[2].wait()
    for dz in range(depth):
        for dr in (0, 1):
            if (dr, dz) != (0, 0):
                to = peer(dr, dz)
                cols = pl.ds(pl.multiple_of((to[0] * depth + to[1]) * group, group), group)
                extras[dr, dz] = (
                    send(tags, tags_in.at[dr, dz], to),
                    send(residual.at[:, cols], residual_cols.at[dr, dz], to),
                )
    project(mid)
    each(w2.s1, (0,), (1,))
    each(w0.s5)
    each(w1.s3)
    each(w2.s2, (0,), (1,))
    to_tokens(0)
    each(w1.s5)
    each(w2.s3)
    to_tokens(1)
    each(w2.s5)
    to_tokens(2)

    shares = [(0, 16), (16, 8), (24, 8)]
    all_waves = range(len(shares))
    lane = lax.broadcasted_iota(jnp.int32, (1, 16 * depth), 1)
    tag = jnp.zeros((1, 16 * depth), f32)
    for dz in range(depth):
        for dr in (0, 1):
            if (dr, dz) == (0, 0):
                got = tags[...]
            else:
                extras[dr, dz][0].wait_recv()
                got = tags_in[dr, dz]
            tag = jnp.where((lane >> 3) == (-dz % depth) * 2 + dr, got[0:1], tag)
    row, col = table((2 * EXPERTS * 2 * CAP * depth, 16 * depth))
    kind, wave, from_z, place = row >> 5, (row >> 4) & 1, (row & 15) >> 1, row & 1
    token_z = (z + (col >> 4)) & (depth - 1)
    token_wave = (r + ((col >> 3) & 1) + kind // EXPERTS) & 1
    fits = (tag == (kind * CAP + place).astype(f32)) & (token_z == from_z) & (token_wave == wave)
    slots = jnp.dot(jnp.where(fits, 1.0, 0.0).astype(bf16), stack[...], preferred_element_type=f32)
    by_kind = slots.reshape(2 * EXPERTS, 4 * depth, group)
    for w, (low, size) in enumerate(shares):
        outgoing[w][...] = by_kind[:, low : low + size].astype(bf16)
    halves = depth // EXPERTS
    dispatched = {}
    for w in all_waves:
        for dz in range(depth):
            for dr in (0, 1):
                to = peer(dr, dz)
                src = outgoing[w].at[to[0] * EXPERTS + to[1] // halves]
                dst = arrived[w].at[mine]
                dispatched[w, dr, dz] = Local(src, dst) if (dr, dz) == (0, 0) else send(src, dst, to)
    resid_to_tokens()
    for load in loads[3:5]:
        load.wait()

    def tokens():
        squares = jnp.zeros((8, group), f32)
        for dz in range(depth):
            for dr in (0, 1):
                columns[dr, dz].wait_recv()
        for g in range(2 * depth):
            value = heads[g].astype(f32)
            resid[:, g * group : (g + 1) * group] = value
            squares = squares + value * value
        inverse = lax.rsqrt(jnp.sum(squares, axis=1, keepdims=True) / width + EPSILON)
        logits = jnp.zeros((8, group), f32)
        for g in range(2 * depth):
            cols = slice(g * group, (g + 1) * group)
            normed = (resid[:, cols] * inverse * gains_of(g, 8)).astype(bf16).astype(f32)
            picked = jnp.zeros((8, group), f32)
            for e in range(2 * EXPERTS):
                line = router[e // EXPERTS, :, cols].astype(f32)[e % EXPERTS : e % EXPERTS + 1]
                picked = jnp.where(route_rows == e, line, picked)
            logits = logits + normed * picked
        return jax.nn.sigmoid(jnp.sum(logits, axis=1, keepdims=True))

    lanes = gain.shape[1]
    per_group = group // lanes

    def gains_of(g, lines):
        rows_of = gain[pl.ds(g // 2 * 2 * per_group, 2 * per_group), :].astype(f32)
        first = g % 2 * per_group
        return jnp.concatenate(
            [jnp.broadcast_to(rows_of[first + k : first + k + 1], (lines, lanes)) for k in range(per_group)], axis=1
        )

    side_sent = [{} for _ in all_waves]
    gathers = [Gather(send, near, grid[w], fold_cols, twin) for w in all_waves]
    sums = [Sums(send, near, *part[w][:6], part[w][7], side_sent[w]) for w in all_waves]

    def enter(w):
        lines = shares[w][1]
        squares = jnp.zeros((lines, group), f32)
        for dz in range(depth):
            for dr in (0, 1):
                dispatched[w, dr, dz].wait_recv()
        for g in range(2 * depth):
            value = arrived[w][g].astype(f32)
            squares = squares + value * value
        inverse = lax.rsqrt(jnp.sum(squares, axis=1, keepdims=True) / width + EPSILON)
        for g in range(2 * depth):
            normed = (arrived[w][g].astype(f32) * inverse * gains_of(g, lines)).astype(bf16)
            at = g * group
            if g < 4:
                at = lax.rem(parity + g // 2, 2) * fold_cols + g % 2 * group
                at = pl.multiple_of(at, group)
            grid[w][0, 0, :, pl.ds(at, group)] = normed
        gathers[w].begin()

    chunk = width // 16

    def up_piece(w, low, high):
        many = SIDE * SIDE * shares[w][1]
        total = acc.at[pl.ds(0, many)]
        if low == 0:
            total[...] = jnp.zeros((many, acc.shape[1]), f32)

        def body(i, _):
            at = pl.ds(pl.multiple_of(i * chunk, chunk), chunk)
            lines = grid[w][:, :, :, at]
            if shares[w][1] % 16:
                lines = lines.astype(f32).reshape(many, chunk).astype(bf16)
            else:
                lines = lines.reshape(many, chunk)
            total[...] += jnp.dot(lines, up[at, :], preferred_element_type=f32)
            return 0

        lax.fori_loop(low, high, body, 0)
        if high == 16:
            hidden[pl.ds(0, many), :] = jax.nn.gelu(total[...]).astype(bf16)

    def product(w, at):
        lines = shares[w][1]
        got = jnp.dot(hidden[pl.ds(0, 16 * lines), :], down[:, at], preferred_element_type=f32)
        return got.reshape(SIDE, SIDE, lines, got.shape[1]).astype(bf16)

    def down_side(w):
        side_chunk = fold_cols // 2
        side_out, side_in = part[w][6:]

        def body(i, _):
            at = pl.ds(pl.multiple_of(i * side_chunk, side_chunk), side_chunk)
            got = product(w, at)
            for k in range(SIDE):
                side_out[k, :, :, at] = got[:, k]
            return 0

        lax.fori_loop(0, 2, body, 0)
        for k in (2, 3, 1, 0):
            side_sent[w][k] = send(side_out.at[k], side_in.at[k], twin)

    out_chunk = (width - fold_cols) // 4 // 7

    def down_piece(w, quarter):
        def body(i, _):
            here = pl.ds(pl.multiple_of(i * out_chunk, out_chunk), out_chunk)
            at = pl.ds(pl.multiple_of(fold_cols + (quarter * 7 + i) * out_chunk, out_chunk), out_chunk)
            part[w][0][quarter, :, :, :, here] = product(w, at)
            return 0

        lax.fori_loop(0, 7, body, 0)

    def down_and_send(w, h, quarter):
        down_piece(w, 2 * h + quarter)
        sums[w].s1(h, quarter)

    returns = {}
    landed = [rsem.at[NSEM - depth + k] for k in range(depth)]
    my_landed = rsem.at[NSEM - depth + z]

    def leave(w):
        total = jnp.concatenate([sums[w].s6(h) for h in (0, 1)], axis=1)
        mine_too = total[:, :fold_cols]
        lines = [jnp.where(parity == k, 0.0, mine_too) for k in (0, 1)]
        lines += [total[:, j * fold_cols : (j + 1) * fold_cols] for j in range(1, 7)]
        block = jnp.concatenate(lines, axis=0).astype(bf16)
        by = fold if w == 0 else fold_small
        sorted_lines = jnp.dot(by[...], block, preferred_element_type=f32).astype(bf16)
        back[w][...] = sorted_lines.reshape(back[w].shape)
        dst = returned.at[mine]
        if w == 0:
            for dz in range(depth):
                src = back[0].at[lax.rem(z - dz + depth, depth)]
                returns[dz] = Local(src, dst) if dz == 0 else send(src, dst, peer(0, -dz))
        else:
            for k in range(depth // 2):
                to = (lax.rem(r + 1, 2), (w - 1) * (depth // 2) + k, t)
                returns[w, k] = send(back[w].at[k], dst, to, my_landed)

    g0, g1, g2 = gathers
    v0, v1, v2 = sums
    enter(0)
    each(g0.step1)
    each(g0.onward, (0,))
    each(g0.step3)
    enter(1)
    each(g0.onward, (3,), (1,))
    g0.last(0)
    enter(2)
    each(g1.step1)
    each(g0.onward, (2,))
    g0.last(3)
    g0.last(1)
    each(g1.onward, (0,))
    each(g2.step1)
    g0.last(2)
    g0.end()
    for i in (5, 7, 9):
        loads[i].wait()
    up_piece(0, 0, 4)
    each(g1.step3)
    each(g2.onward, (0,))
    up_piece(0, 4, 8)
    each(g1.onward, (3,), (1,))
    each(g2.step3)
    g1.last(0)
    up_piece(0, 8, 12)
    each(g1.onward, (2,))
    g1.last(3)
    g1.last(1)
    each(g2.onward, (3,))
    up_piece(0, 12, 16)
    each(g2.onward, (1,))
    g2.last(0)
    g1.last(2)
    for i in (6, 8, 10):
        loads[i].wait()
    down_side(0)
    down_and_send(0, 1, 0)
    each(g2.onward, (2,))
    g2.last(3)
    g2.last(1)
    down_and_send(0, 0, 1)
    g1.end()
    down_and_send(0, 1, 1)
    g2.last(2)
    down_piece(0, 0)
    up_piece(1, 0, 8)
    v0.s2(1, 0)
    v0.s1(0, 0)
    up_piece(1, 8, 16)
    v0.s2(0, 1)
    v0.s2(1, 1)
    g2.end()
    down_side(1)
    down_and_send(1, 1, 0)
    down_and_send(1, 0, 1)
    v0.s2(0, 0)
    down_and_send(1, 1, 1)
    down_piece(1, 0)
    v0.s3(1)
    up_piece(2, 0, 8)
    v1.s1(0, 0)
    v1.s2(1, 0)
    up_piece(2, 8, 16)
    v0.s3(0)
    down_side(2)
    down_and_send(2, 1, 0)
    v1.s2(0, 1)
    down_and_send(2, 0, 1)
    v1.s2(1, 1)
    down_and_send(2, 1, 1)
    down_piece(2, 0)
    v0.s5(1)
    v1.s2(0, 0)
    v0.s5(0)
    gating = tokens()
    v1.s3(1)
    v2.s1(0, 0)
    v2.s2(1, 0)
    leave(0)
    v1.s3(0)
    v2.s2(0, 1)
    v1.s5(1)
    v2.s2(1, 1)
    v1.s5(0)
    v2.s2(0, 0)
    v2.s3(1)
    leave(1)
    v2.s5(1)
    v2.s3(0)
    v2.s5(0)
    leave(2)
    for dz in range(depth):
        returns[dz].wait_recv()
    for k in range(depth):
        pltpu.make_async_copy(back[1].at[0], returned.at[0], landed[k]).wait()
    block = returned[...].reshape(2 * depth * 8 * CAP, fold_cols)
    experts = jnp.dot(put[...], block, preferred_element_type=f32)
    for j in range(8):
        cols = slice(j * fold_cols, (j + 1) * fold_cols)
        out[:, cols] = (resid[:, cols] + gating * experts[j * 8 : j * 8 + 8]).astype(bf16)
    for copy in sent:
        copy.wait_send()
    assert count[0] <= NSEM - depth


def per_device(
    residual_in, context, out_weight, norm_gain, router, up_weight, down_weight, modality, expert
):
    tok_rows, width = residual_in.shape
    depth = lax.axis_size("exp")
    hidden_units = up_weight.shape[3]
    fold_cols = width // 8
    slot_rows = CAP * depth
    kinds = 2 * EXPERTS
    rows, group = context.shape[0], out_weight.shape[1]
    q = (width - fold_cols) // 4
    g4 = group // 4
    vm = pltpu.VMEM

    def sum_buffers(lines, cols):
        return [
            vm((4, 4, 4, lines, cols), bf16),
            vm((4, 4, lines, cols), bf16),
            vm((2, 2, 2, 4, lines, cols), bf16),
            vm((2, 2, 4, lines, cols), bf16),
            vm((4, lines, cols), bf16),
            vm((2, 2, 2, lines, cols), bf16),
        ]

    scratch = [
        vm((tok_rows, width), bf16),
        vm(out_weight.shape, bf16),
        vm((width // 128, 128), bf16),
        vm(router.shape, bf16),
        vm((8 * tok_rows, 2 * depth * CAP * 8), bf16),
        vm((8 * slot_rows, 8 * slot_rows), bf16),
        vm((4 * slot_rows, 4 * slot_rows), bf16),
        vm((8, 128), f32),
        vm((2, depth, 8, 128), f32),
        vm((2, depth, tok_rows, group), bf16),
        vm((depth, 2, rows, context.shape[1]), bf16),
        vm((2 * rows, group), f32),
        [sum_buffers(48, g4), sum_buffers(32, g4), sum_buffers(48, g4)],
        vm((16 * depth, group), bf16),
        vm((2 * depth, tok_rows, group), bf16),
        vm((2 * depth, tok_rows, group), bf16),
        vm((tok_rows, width), f32),
        [vm((kinds, n, group), bf16) for n in (16, 8, 8)],
        [vm((2 * depth, n, group), bf16) for n in (16, 8, 8)],
        [vm((4, 4, n, width), bf16) for n in (16, 8, 8)],
        vm((width, hidden_units), bf16),
        vm((hidden_units, width), bf16),
        vm((16 * slot_rows, hidden_units), f32),
        vm((16 * slot_rows, hidden_units), bf16),
        [
            sum_buffers(n, q) + [vm((4, 4, n, fold_cols), bf16), vm((4, 4, n, fold_cols), bf16)]
            for n in (16, 8, 8)
        ],
        [vm((n, CAP * 8, fold_cols), bf16) for n in (8, 4, 4)],
        vm((2 * depth, CAP * 8, fold_cols), bf16),
        pltpu.SemaphoreType.DMA((NSEM,)),
        pltpu.SemaphoreType.DMA((NSEM,)),
        pltpu.SemaphoreType.DMA((11,)),
    ]
    local = pl.BlockSpec(memory_space=pltpu.VMEM)
    there = pl.BlockSpec(memory_space=pl.ANY)
    return pl.pallas_call(
        functools.partial(kernel, depth),
        out_shape=jax.ShapeDtypeStruct((tok_rows, width), bf16),
        in_specs=[pl.BlockSpec(memory_space=pltpu.SMEM)] * 2 + [there] * 7,
        out_specs=local,
        scratch_shapes=scratch,
        compiler_params=pltpu.CompilerParams(
            collective_id=0, has_side_effects=True, vmem_limit_bytes=63_000_000
        ),
    )(
        modality,
        expert,
        residual_in,
        context,
        out_weight,
        norm_gain.reshape(width // 128, 128),
        router,
        up_weight.reshape(width, hidden_units),
        down_weight.reshape(hidden_units, width),
    )


def solution(mesh):
    in_specs = (
        P(("role", "exp", "tp"), None),
        P(("role", "exp"), "tp"),
        P("tp", ("role", "exp")),
        P(),
        P(),
        P("role", "exp", None, "tp"),
        P("role", "exp", "tp", None),
        P(("role", "exp", "tp")),
        P(("role", "exp", "tp")),
    )
    out_specs = P(("role", "exp", "tp"), None)
    return jax.shard_map(
        per_device, mesh=mesh, in_specs=in_specs, out_specs=out_specs, check_vma=False
    )
```

```python
import functools

import jax
import jax.numpy as jnp
from jax import lax
from jax.experimental import pallas as pl
from jax.experimental.pallas import tpu as pltpu
from jax.sharding import PartitionSpec as P

EXPERTS = 4
CAP = 2
EPSILON = 1e-05
SIDE = 4
NSEM = 496
f32, bf16 = jnp.float32, jnp.bfloat16
MESH = pl.DeviceIdType.MESH


class Sums:
    def __init__(self, send, near, src, q, f, s, q2, f2, side=None, arrivals=None):
        self.send, self.near, self.side, self.arrivals = send, near, side, arrivals
        self.src, self.q, self.f, self.s, self.q2, self.f2 = src, q, f, s, q2, f2
        self.m, self.n = {}, {}

    def sel(self, h, k, quarter):
        at = 2 * h + quarter
        return self.src.at[at, :, k] if h == 0 else self.src.at[at, k]

    def add_side(self, h, quarter, *ks):
        if self.side is None or (h, quarter) != (0, 0):
            return
        cols = pl.ds(0, self.side.shape[3])
        for k in ks:
            self.arrivals[k].wait_recv()

            def body(i, _, k=k):
                was = self.src[0, i, k, :, cols].astype(f32)
                self.src[0, i, k, :, cols] = (was + self.side[k, i].astype(f32)).astype(bf16)
                return 0

            lax.fori_loop(0, SIDE, body, 0)

    def s1(self, h, quarter):
        self.add_side(h, quarter, 2, 3)
        plus, minus = self.near(1 - h, 1), self.near(1 - h, -1)
        if quarter == 0:
            self.m[h, 1] = self.send(self.sel(h, 2, 0), self.q.at[h * 2], plus)
            self.m[h, 4] = self.send(self.sel(h, 3, 0), self.f.at[h, 1, 0], minus)
        else:
            self.m[h, 2] = self.send(self.sel(h, 2, 1), self.q.at[h * 2 + 1], minus)
            self.m[h, 3] = self.send(self.sel(h, 1, 1), self.f.at[h, 0, 1], plus)

    def s2(self, h, quarter):
        k, which = (1, 1) if quarter == 0 else (3, 2)
        at = 2 * h + quarter
        got = self.q.at[at]
        self.add_side(h, quarter, 1)
        self.m[h, which].wait_recv()

        def body(i, _):
            where = (at, i, k) if h == 0 else (at, k, i)
            self.src[where] = (self.src[where].astype(f32) + got[i].astype(f32)).astype(bf16)
            return 0

        lax.fori_loop(0, SIDE, body, 0)
        if quarter == 0:
            self.m[h, 5] = self.send(self.sel(h, 1, 0), self.f.at[h, 0, 0], self.near(1 - h, 1))
        else:
            self.m[h, 6] = self.send(self.sel(h, 3, 1), self.f.at[h, 1, 1], self.near(1 - h, -1))

    def s3(self, h):
        self.add_side(h, 0, 0)
        for i in (3, 4, 5, 6):
            self.m[h, i].wait_recv()

        def body(i, _):
            for quarter in (0, 1):
                at = 2 * h + quarter
                where = (at, i, 0) if h == 0 else (at, 0, i)
                total = self.src[where].astype(f32) + self.f[h, 0, quarter, i].astype(f32)
                self.s[h, quarter, i] = (total + self.f[h, 1, quarter, i].astype(f32)).astype(bf16)
            return 0

        lax.fori_loop(0, SIDE, body, 0)
        plus, minus = self.near(h, 1), self.near(h, -1)
        self.n[h, 1] = self.send(self.s.at[h, 0, 2], self.q2.at[h * 2], plus)
        self.n[h, 2] = self.send(self.s.at[h, 1, 2], self.q2.at[h * 2 + 1], minus)
        self.n[h, 3] = self.send(self.s.at[h, 1, 1], self.f2.at[h, 0, 1], plus)
        self.n[h, 4] = self.send(self.s.at[h, 0, 3], self.f2.at[h, 1, 0], minus)

    def s5(self, h):
        self.n[h, 1].wait_recv()
        self.s[h, 0, 1] = (self.s[h, 0, 1].astype(f32) + self.q2[h * 2].astype(f32)).astype(bf16)
        self.n[h, 5] = self.send(self.s.at[h, 0, 1], self.f2.at[h, 0, 0], self.near(h, 1))
        self.n[h, 2].wait_recv()
        self.s[h, 1, 3] = (self.s[h, 1, 3].astype(f32) + self.q2[h * 2 + 1].astype(f32)).astype(bf16)
        self.n[h, 6] = self.send(self.s.at[h, 1, 3], self.f2.at[h, 1, 1], self.near(h, -1))

    def s6(self, h):
        for i in (3, 4, 5, 6):
            self.n[h, i].wait_recv()
        parts = []
        for quarter in (0, 1):
            total = self.s[h, quarter, 0].astype(f32) + self.f2[h, 0, quarter].astype(f32)
            parts.append(total + self.f2[h, 1, quarter].astype(f32))
        return jnp.concatenate(parts, axis=1)


class Gather:
    def __init__(self, send, near, dst, base, twin):
        self.send, self.near, self.dst, self.base, self.twin = send, near, dst, base, twin
        self.part = (dst.shape[3] - base) // 4
        self.m = {}

    def blk(self, h, a, b, c, w):
        i, j = (a, b) if h == 0 else (b, a)
        return self.dst.at[i, j, :, pl.ds(self.base + h * 2 * self.part + c, w)]

    def first(self, h, name, a, b, c, w, sign, a2):
        self.m[h, name] = self.send(self.blk(h, a, b, c, w), self.blk(h, a2, b, c, w), self.near(h, sign))

    def second(self, h, name, a, b, c, w, sign, b2):
        self.m[h, name] = self.send(self.blk(h, a, b, c, w), self.blk(h, a, b2, c, w), self.near(1 - h, sign))

    def over(self, h, a, b):
        if h == 0:
            near, far = self.dst.at[a, b, :, pl.ds(self.base, self.base)], self.dst.at[a, b, :, pl.ds(0, self.base)]
            self.m["z", a, b] = self.send(near, far, self.twin)

    def across(self, h, a):
        p = self.part
        self.second(h, ("p", a), a, 0, 0, 2 * p, 1, 3)
        self.second(h, ("m", a), a, 0, 0, 2 * p, -1, 1)

    def begin(self):
        p = self.part
        for h in (0, 1):
            self.first(h, "p", 0, 0, 0, 2 * p, 1, 3)
            self.first(h, "m", 0, 0, 0, 2 * p, -1, 1)
        for h in (0, 1):
            self.across(h, 0)

    def step1(self, h):
        p = self.part
        self.m[h, "p"].wait_recv()
        self.first(h, "pp", 3, 0, 0, p, 1, 2)
        self.m[h, "m"].wait_recv()
        self.first(h, "mm", 1, 0, p, p, -1, 2)
        self.across(h, 3)
        self.across(h, 1)
        self.over(h, 3, 0)
        self.over(h, 1, 0)

    def onward(self, h, a):
        p = self.part
        self.m[h, ("p", a)].wait_recv()
        self.second(h, ("pp", a), a, 3, 0, p, 1, 2)
        self.m[h, ("m", a)].wait_recv()
        self.second(h, ("mm", a), a, 1, p, p, -1, 2)
        self.over(h, a, 3)
        self.over(h, a, 1)

    def step3(self, h):
        self.m[h, "pp"].wait_recv()
        self.m[h, "mm"].wait_recv()
        self.across(h, 2)
        self.over(h, 2, 0)

    def last(self, a):
        for h in (0, 1):
            self.m[h, ("pp", a)].wait_recv()
            self.m[h, ("mm", a)].wait_recv()
            self.over(h, a, 2)

    def end(self):
        for a in range(SIDE):
            for b in range(SIDE):
                if (a, b) != (0, 0):
                    self.m["z", a, b].wait_recv()


def kernel(
    depth, modality, expert, residual_in, context, out_weight_in, gain_in, router_in, up_hbm, down_hbm, out,
    residual, out_weight, gain, router, put, fold, fold_small, tags, tags_in, residual_cols, cg, res, wave_bufs, stack, tiles, heads,
    resid, outgoing, arrived, grid, up, down, acc, hidden, part, back, returned, ssem, rsem, wsem,
):
    r, z, t = lax.axis_index("role"), lax.axis_index("exp"), lax.axis_index("tp")
    x, y = t // SIDE, t % SIDE
    width = out.shape[1]
    fold_cols = width // 8
    count = [0]
    sent = []

    def send(src, dst, device, landed=None):
        k = count[0]
        count[0] += 1
        copy = pltpu.make_async_remote_copy(
            src_ref=src,
            dst_ref=dst,
            send_sem=ssem.at[k],
            recv_sem=rsem.at[k] if landed is None else landed,
            device_id=device,
            device_id_type=MESH,
        )
        copy.start()
        sent.append(copy)
        return copy

    class Local:
        def __init__(self, src, dst):
            k = count[0]
            count[0] += 1
            self.copy = pltpu.make_async_copy(src, dst, rsem.at[k])
            self.copy.start()

        def wait_recv(self):
            self.copy.wait()

    def near(axis, step):
        if axis == 0:
            return (r, z, lax.rem(x + step + SIDE, SIDE) * SIDE + y)
        return (r, z, x * SIDE + lax.rem(y + step + SIDE, SIDE))

    def peer(dr, dz):
        return (lax.rem(r + dr, 2), lax.rem(z + dz + depth, depth), t)

    mid = depth // 2
    parity = lax.rem(z, 2)
    twin = (r, z + 1 - 2 * parity, t)
    barrier = pltpu.get_barrier_semaphore()
    others = [peer(1, 0), peer(0, 1), peer(0, -1)]
    others += [near(axis, step) for axis in (0, 1) for step in (1, -1)]
    for device in others:
        pl.semaphore_signal(barrier, inc=1, device_id=device, device_id_type=MESH)
    pairs = [(context, cg.at[0, 0]), (out_weight_in, out_weight), (residual_in, residual), (gain_in, gain),
             (router_in, router)]
    for k, at in enumerate([parity, 1 - parity]):
        here, there = pl.ds(k * fold_cols, fold_cols), pl.ds(pl.multiple_of(at * fold_cols, fold_cols), fold_cols)
        pairs += [(up_hbm.at[there], up.at[here]), (down_hbm.at[:, there], down.at[:, here])]
    rest = pl.ds(2 * fold_cols, width - 2 * fold_cols)
    pairs += [(up_hbm.at[rest], up.at[rest]), (down_hbm.at[:, rest], down.at[:, rest])]
    loads = [pltpu.make_async_copy(src, dst, wsem.at[i]) for i, (src, dst) in enumerate(pairs)]
    for load in loads:
        load.start()

    routes = [modality[i] * EXPERTS + expert[i] for i in range(8)]
    slot_of = []
    for i in range(8):
        place = routes[i] * CAP
        for k in range(i):
            place = place + jnp.where(routes[k] == routes[i], 1, 0)
        slot_of.append(place)

    def spread(values, index):
        total = jnp.zeros(index.shape, jnp.int32)
        for i, value in enumerate(values):
            total = jnp.where(index == i, value, total)
        return total

    def table(shape):
        return (lax.broadcasted_iota(jnp.int32, shape, 0), lax.broadcasted_iota(jnp.int32, shape, 1))

    row, col = table(put.shape)
    slot = (col >> 5) * 2 + ((col >> 3) & 1)
    put[...] = jnp.where((slot == spread(slot_of, row & 7)) & ((col & 7) == (row >> 3)), 1.0, 0.0).astype(bf16)
    row, col = table(fold.shape)
    fold[...] = jnp.where(((col & 15) >> 1) * 16 + (col & 1) * 8 + (col >> 4) == row, 1.0, 0.0).astype(bf16)
    row, col = table(fold_small.shape)
    fold_small[...] = jnp.where(((col & 7) >> 1) * 16 + (col & 1) * 8 + (col >> 3) == row, 1.0, 0.0).astype(bf16)
    row, col = table((8, 1))
    route_rows = spread(routes, row)
    tags[...] = spread(slot_of, table(tags.shape)[1] & 7).astype(f32)
    loads[0].wait()
    pl.semaphore_wait(barrier, len(others))

    rows = cg.shape[2]
    half_rows = rows // 2
    partner, up_z, down_z = peer(1, 0), peer(0, 1), peer(0, -1)
    piece = [pl.ds(0, half_rows), pl.ds(half_rows, half_rows)]

    def pass_on(a, b, c, device):
        return send(cg.at[a, 0, piece[c]], cg.at[b, 0, piece[c]], device)

    def hand_over(a, c):
        return send(cg.at[a, 0, piece[c]], cg.at[a, 1, piece[c]], partner)

    going = {0: pass_on(0, depth - 1, 0, up_z)}
    coming = {0: pass_on(0, 1, 0, down_z)}
    shared = {0: [send(cg.at[0, 0], cg.at[0, 1], partner)]}
    going[1] = pass_on(0, depth - 1, 1, up_z)
    coming[1] = pass_on(0, 1, 1, down_z)
    loads[1].wait()

    wide = out_weight.shape[1] // 4
    waves = [[0, 1, depth - 1], [2, depth - 2], [3, depth - 3, mid]]
    order = [dz for wave in waves for dz in wave]

    def project(dz):
        for copy in shared[dz]:
            copy.wait_recv()
        k = [dz in wave for wave in waves].index(True)
        p1, low = wave_bufs[k][0], waves[k].index(dz) * 16
        both = jnp.concatenate([cg[dz, 0], cg[dz, 1]], axis=0)
        res[...] = jnp.dot(both, out_weight[...], preferred_element_type=f32)

        def body(i, _):
            dx, dy = i // SIDE, i % SIDE
            home = lax.rem(x + dx, SIDE) * SIDE + lax.rem(y + dy, SIDE)
            at = pl.multiple_of(home * 8, 8)
            block = jnp.concatenate([res[pl.ds(at, 8), :], res[pl.ds(rows + at, 8), :]], axis=0)
            for quarter in range(4):
                cols = slice(quarter * wide, (quarter + 1) * wide)
                p1[quarter, dx, dy, pl.ds(low, 16), :] = block[:, cols].astype(bf16)
            return 0

        lax.fori_loop(0, SIDE * SIDE, body, 0)

    def ring_step(step):
        nonlocal going, coming
        a, b = depth - step, step
        shared[a], shared[b] = [], []
        going_next, coming_next = {}, {}
        for c in (0, 1):
            going[c].wait_recv()
            if step < mid - 1 or c == 0:
                going_next[c] = pass_on(a, a - 1, c, up_z)
            coming[c].wait_recv()
            if step < mid - 1 or c == 1:
                coming_next[c] = pass_on(b, b + 1, c, down_z)
            shared[a].append(hand_over(a, c))
            shared[b].append(hand_over(b, c))
        going, coming = going_next, coming_next

    early = [Sums(send, near, *buffers) for buffers in wave_bufs]
    both_halves = (0, 1)

    def each(step, *rest):
        for args in rest or ((),):
            for h in both_halves:
                step(h, *args)

    mine = r * depth + z
    columns, extras = {}, {}
    group = width // (2 * depth)

    def to_tokens(k):
        final = [early[k].s6(h) for h in both_halves]
        for i, dz in enumerate(waves[k]):
            pair = []
            for dr in (0, 1):
                at = slice(i * 16 + dr * 8, i * 16 + dr * 8 + 8)
                if dz == 0 and dr == 0:
                    cols = pl.ds(pl.multiple_of(mine * group, group), group)
                    own = residual[:, cols].astype(f32)
                else:
                    extras[dr, -dz % depth][1].wait_recv()
                    own = residual_cols[dr, -dz % depth].astype(f32)
                value = (own + jnp.concatenate([final[0][at], final[1][at]], axis=1)).astype(bf16)
                tiles[dz * 2 + dr] = value
                pair.append(value.astype(f32))
            stack[pl.ds(dz * 16, 16), :] = jnp.concatenate(pair, axis=0).astype(bf16)

    def resid_to_tokens():
        for dz in range(depth):
            for dr in (0, 1):
                src, dst = tiles.at[dz * 2 + dr], heads.at[mine]
                columns[dr, dz] = Local(src, dst) if (dr, dz) == (0, 0) else send(src, dst, peer(dr, dz))

    w0, w1, w2 = early
    ring_step(1)
    project(0)
    project(depth - 1)
    project(1)
    each(w0.s1, (0,), (1,))
    ring_step(2)
    project(depth - 2)
    project(2)
    each(w1.s1, (0,), (1,))
    each(w0.s2, (0,), (1,))
    ring_step(3)
    project(depth - 3)
    project(3)
    each(w0.s3)
    going[0].wait_recv()
    shared[mid] = [hand_over(mid, 0)]
    coming[1].wait_recv()
    shared[mid].append(hand_over(mid, 1))
    each(w1.s2, (0,), (1,))
    project(mid)
    loads[2].wait()
    for dz in range(depth):
        for dr in (0, 1):
            if (dr, dz) != (0, 0):
                to = peer(dr, dz)
                cols = pl.ds(pl.multiple_of((to[0] * depth + to[1]) * group, group), group)
                extras[dr, dz] = (
                    send(tags, tags_in.at[dr, dz], to),
                    send(residual.at[:, cols], residual_cols.at[dr, dz], to),
                )
    each(w2.s1, (0,), (1,))
    each(w0.s5)
    each(w1.s3)
    each(w2.s2, (0,), (1,))
    to_tokens(0)
    each(w1.s5)
    each(w2.s3)
    to_tokens(1)
    each(w2.s5)
    to_tokens(2)

    shares = [(0, 16), (16, 8), (24, 8)]
    all_waves = range(len(shares))
    lane = lax.broadcasted_iota(jnp.int32, (1, 16 * depth), 1)
    tag = jnp.zeros((1, 16 * depth), f32)
    for dz in range(depth):
        for dr in (0, 1):
            if (dr, dz) == (0, 0):
                got = tags[...]
            else:
                extras[dr, dz][0].wait_recv()
                got = tags_in[dr, dz]
            tag = jnp.where((lane >> 3) == (-dz % depth) * 2 + dr, got[0:1], tag)
    row, col = table((2 * EXPERTS * 2 * CAP * depth, 16 * depth))
    kind, wave, from_z, place = row >> 5, (row >> 4) & 1, (row & 15) >> 1, row & 1
    token_z = (z + (col >> 4)) & (depth - 1)
    token_wave = (r + ((col >> 3) & 1) + kind // EXPERTS) & 1
    fits = (tag == (kind * CAP + place).astype(f32)) & (token_z == from_z) & (token_wave == wave)
    slots = jnp.dot(jnp.where(fits, 1.0, 0.0).astype(bf16), stack[...], preferred_element_type=f32)
    by_kind = slots.reshape(2 * EXPERTS, 4 * depth, group)
    for w, (low, size) in enumerate(shares):
        outgoing[w][...] = by_kind[:, low : low + size].astype(bf16)
    halves = depth // EXPERTS
    dispatched = {}
    for w in all_waves:
        for dz in range(depth):
            for dr in (0, 1):
                to = peer(dr, dz)
                src = outgoing[w].at[to[0] * EXPERTS + to[1] // halves]
                dst = arrived[w].at[mine]
                dispatched[w, dr, dz] = Local(src, dst) if (dr, dz) == (0, 0) else send(src, dst, to)
    resid_to_tokens()
    for load in loads[3:5]:
        load.wait()

    def tokens():
        squares = jnp.zeros((8, group), f32)
        for dz in range(depth):
            for dr in (0, 1):
                columns[dr, dz].wait_recv()
        for g in range(2 * depth):
            value = heads[g].astype(f32)
            resid[:, g * group : (g + 1) * group] = value
            squares = squares + value * value
        inverse = lax.rsqrt(jnp.sum(squares, axis=1, keepdims=True) / width + EPSILON)
        logits = jnp.zeros((8, group), f32)
        for g in range(2 * depth):
            cols = slice(g * group, (g + 1) * group)
            normed = (resid[:, cols] * inverse * gains_of(g, 8)).astype(bf16).astype(f32)
            picked = jnp.zeros((8, group), f32)
            for e in range(2 * EXPERTS):
                line = router[e // EXPERTS, :, cols].astype(f32)[e % EXPERTS : e % EXPERTS + 1]
                picked = jnp.where(route_rows == e, line, picked)
            logits = logits + normed * picked
        return jax.nn.sigmoid(jnp.sum(logits, axis=1, keepdims=True))

    lanes = gain.shape[1]
    per_group = group // lanes

    def gains_of(g, lines):
        rows_of = gain[pl.ds(g // 2 * 2 * per_group, 2 * per_group), :].astype(f32)
        first = g % 2 * per_group
        return jnp.concatenate(
            [jnp.broadcast_to(rows_of[first + k : first + k + 1], (lines, lanes)) for k in range(per_group)], axis=1
        )

    side_sent = [{} for _ in all_waves]
    gathers = [Gather(send, near, grid[w], fold_cols, twin) for w in all_waves]
    sums = [Sums(send, near, *part[w][:6], part[w][7], side_sent[w]) for w in all_waves]

    def enter(w):
        lines = shares[w][1]
        squares = jnp.zeros((lines, group), f32)
        for dz in range(depth):
            for dr in (0, 1):
                dispatched[w, dr, dz].wait_recv()
        for g in range(2 * depth):
            value = arrived[w][g].astype(f32)
            squares = squares + value * value
        inverse = lax.rsqrt(jnp.sum(squares, axis=1, keepdims=True) / width + EPSILON)
        for g in range(2 * depth):
            normed = (arrived[w][g].astype(f32) * inverse * gains_of(g, lines)).astype(bf16)
            at = g * group
            if g < 4:
                at = lax.rem(parity + g // 2, 2) * fold_cols + g % 2 * group
                at = pl.multiple_of(at, group)
            grid[w][0, 0, :, pl.ds(at, group)] = normed
        gathers[w].begin()

    chunk = width // 16

    def up_piece(w, low, high):
        many = SIDE * SIDE * shares[w][1]
        total = acc.at[pl.ds(0, many)]
        if low == 0:
            total[...] = jnp.zeros((many, acc.shape[1]), f32)

        def body(i, _):
            at = pl.ds(pl.multiple_of(i * chunk, chunk), chunk)
            lines = grid[w][:, :, :, at]
            if shares[w][1] % 16:
                lines = lines.astype(f32).reshape(many, chunk).astype(bf16)
            else:
                lines = lines.reshape(many, chunk)
            total[...] += jnp.dot(lines, up[at, :], preferred_element_type=f32)
            return 0

        lax.fori_loop(low, high, body, 0)
        if high == 16:
            hidden[pl.ds(0, many), :] = jax.nn.gelu(total[...]).astype(bf16)

    def product(w, at):
        lines = shares[w][1]
        got = jnp.dot(hidden[pl.ds(0, 16 * lines), :], down[:, at], preferred_element_type=f32)
        return got.reshape(SIDE, SIDE, lines, got.shape[1]).astype(bf16)

    def down_side(w):
        side_chunk = fold_cols // 2
        side_out, side_in = part[w][6:]

        def body(i, _):
            at = pl.ds(pl.multiple_of(i * side_chunk, side_chunk), side_chunk)
            got = product(w, at)
            for k in range(SIDE):
                side_out[k, :, :, at] = got[:, k]
            return 0

        lax.fori_loop(0, 2, body, 0)
        for k in (2, 3, 1, 0):
            side_sent[w][k] = send(side_out.at[k], side_in.at[k], twin)

    out_chunk = (width - fold_cols) // 4 // 7

    def down_piece(w, quarter):
        def body(i, _):
            here = pl.ds(pl.multiple_of(i * out_chunk, out_chunk), out_chunk)
            at = pl.ds(pl.multiple_of(fold_cols + (quarter * 7 + i) * out_chunk, out_chunk), out_chunk)
            part[w][0][quarter, :, :, :, here] = product(w, at)
            return 0

        lax.fori_loop(0, 7, body, 0)

    def down_and_send(w, h, quarter):
        down_piece(w, 2 * h + quarter)
        sums[w].s1(h, quarter)

    returns = {}
    landed = [rsem.at[NSEM - depth + k] for k in range(depth)]
    my_landed = rsem.at[NSEM - depth + z]

    def leave(w):
        total = jnp.concatenate([sums[w].s6(h) for h in (0, 1)], axis=1)
        mine_too = total[:, :fold_cols]
        lines = [jnp.where(parity == k, 0.0, mine_too) for k in (0, 1)]
        lines += [total[:, j * fold_cols : (j + 1) * fold_cols] for j in range(1, 7)]
        block = jnp.concatenate(lines, axis=0).astype(bf16)
        by = fold if w == 0 else fold_small
        sorted_lines = jnp.dot(by[...], block, preferred_element_type=f32).astype(bf16)
        back[w][...] = sorted_lines.reshape(back[w].shape)
        dst = returned.at[mine]
        if w == 0:
            for dz in range(depth):
                src = back[0].at[lax.rem(z - dz + depth, depth)]
                returns[dz] = Local(src, dst) if dz == 0 else send(src, dst, peer(0, -dz))
        else:
            for k in range(depth // 2):
                to = (lax.rem(r + 1, 2), (w - 1) * (depth // 2) + k, t)
                returns[w, k] = send(back[w].at[k], dst, to, my_landed)

    g0, g1, g2 = gathers
    v0, v1, v2 = sums
    enter(0)
    each(g0.step1)
    each(g0.onward, (0,))
    each(g0.step3)
    enter(1)
    each(g0.onward, (3,), (1,))
    g0.last(0)
    enter(2)
    each(g1.step1)
    each(g0.onward, (2,))
    g0.last(3)
    g0.last(1)
    each(g1.onward, (0,))
    each(g2.step1)
    g0.last(2)
    g0.end()
    for i in (5, 7, 9):
        loads[i].wait()
    up_piece(0, 0, 4)
    each(g1.step3)
    each(g2.onward, (0,))
    up_piece(0, 4, 8)
    each(g1.onward, (3,), (1,))
    each(g2.step3)
    g1.last(0)
    up_piece(0, 8, 12)
    each(g1.onward, (2,))
    g1.last(3)
    g1.last(1)
    each(g2.onward, (3,))
    up_piece(0, 12, 16)
    each(g2.onward, (1,))
    g2.last(0)
    g1.last(2)
    for i in (6, 8, 10):
        loads[i].wait()
    down_side(0)
    down_and_send(0, 1, 0)
    each(g2.onward, (2,))
    g2.last(3)
    g2.last(1)
    down_and_send(0, 0, 1)
    g1.end()
    down_and_send(0, 1, 1)
    g2.last(2)
    down_piece(0, 0)
    up_piece(1, 0, 8)
    v0.s2(1, 0)
    v0.s1(0, 0)
    up_piece(1, 8, 16)
    v0.s2(0, 1)
    v0.s2(1, 1)
    g2.end()
    down_side(1)
    down_and_send(1, 1, 0)
    down_and_send(1, 0, 1)
    v0.s2(0, 0)
    down_and_send(1, 1, 1)
    down_piece(1, 0)
    v0.s3(1)
    up_piece(2, 0, 8)
    v1.s1(0, 0)
    v1.s2(1, 0)
    up_piece(2, 8, 16)
    v0.s3(0)
    down_side(2)
    down_and_send(2, 1, 0)
    v1.s2(0, 1)
    down_and_send(2, 0, 1)
    v1.s2(1, 1)
    down_and_send(2, 1, 1)
    down_piece(2, 0)
    v0.s5(1)
    v1.s2(0, 0)
    v0.s5(0)
    v1.s3(1)
    v2.s1(0, 0)
    v2.s2(1, 0)
    leave(0)
    v1.s3(0)
    v2.s2(0, 1)
    v1.s5(1)
    v2.s2(1, 1)
    v1.s5(0)
    v2.s2(0, 0)
    v2.s3(1)
    leave(1)
    v2.s5(1)
    v2.s3(0)
    gating = tokens()
    v2.s5(0)
    leave(2)
    for dz in range(depth):
        returns[dz].wait_recv()
    for k in range(depth):
        pltpu.make_async_copy(back[1].at[0], returned.at[0], landed[k]).wait()
    block = returned[...].reshape(2 * depth * 8 * CAP, fold_cols)
    experts = jnp.dot(put[...], block, preferred_element_type=f32)
    for j in range(8):
        cols = slice(j * fold_cols, (j + 1) * fold_cols)
        out[:, cols] = (resid[:, cols] + gating * experts[j * 8 : j * 8 + 8]).astype(bf16)
    for copy in sent:
        copy.wait_send()
    assert count[0] <= NSEM - depth


def per_device(
    residual_in, context, out_weight, norm_gain, router, up_weight, down_weight, modality, expert
):
    tok_rows, width = residual_in.shape
    depth = lax.axis_size("exp")
    hidden_units = up_weight.shape[3]
    fold_cols = width // 8
    slot_rows = CAP * depth
    kinds = 2 * EXPERTS
    rows, group = context.shape[0], out_weight.shape[1]
    q = (width - fold_cols) // 4
    g4 = group // 4
    vm = pltpu.VMEM

    def sum_buffers(lines, cols):
        return [
            vm((4, 4, 4, lines, cols), bf16),
            vm((4, 4, lines, cols), bf16),
            vm((2, 2, 2, 4, lines, cols), bf16),
            vm((2, 2, 4, lines, cols), bf16),
            vm((4, lines, cols), bf16),
            vm((2, 2, 2, lines, cols), bf16),
        ]

    scratch = [
        vm((tok_rows, width), bf16),
        vm(out_weight.shape, bf16),
        vm((width // 128, 128), bf16),
        vm(router.shape, bf16),
        vm((8 * tok_rows, 2 * depth * CAP * 8), bf16),
        vm((8 * slot_rows, 8 * slot_rows), bf16),
        vm((4 * slot_rows, 4 * slot_rows), bf16),
        vm((8, 128), f32),
        vm((2, depth, 8, 128), f32),
        vm((2, depth, tok_rows, group), bf16),
        vm((depth, 2, rows, context.shape[1]), bf16),
        vm((2 * rows, group), f32),
        [sum_buffers(48, g4), sum_buffers(32, g4), sum_buffers(48, g4)],
        vm((16 * depth, group), bf16),
        vm((2 * depth, tok_rows, group), bf16),
        vm((2 * depth, tok_rows, group), bf16),
        vm((tok_rows, width), f32),
        [vm((kinds, n, group), bf16) for n in (16, 8, 8)],
        [vm((2 * depth, n, group), bf16) for n in (16, 8, 8)],
        [vm((4, 4, n, width), bf16) for n in (16, 8, 8)],
        vm((width, hidden_units), bf16),
        vm((hidden_units, width), bf16),
        vm((16 * slot_rows, hidden_units), f32),
        vm((16 * slot_rows, hidden_units), bf16),
        [
            sum_buffers(n, q) + [vm((4, 4, n, fold_cols), bf16), vm((4, 4, n, fold_cols), bf16)]
            for n in (16, 8, 8)
        ],
        [vm((n, CAP * 8, fold_cols), bf16) for n in (8, 4, 4)],
        vm((2 * depth, CAP * 8, fold_cols), bf16),
        pltpu.SemaphoreType.DMA((NSEM,)),
        pltpu.SemaphoreType.DMA((NSEM,)),
        pltpu.SemaphoreType.DMA((11,)),
    ]
    local = pl.BlockSpec(memory_space=pltpu.VMEM)
    there = pl.BlockSpec(memory_space=pl.ANY)
    return pl.pallas_call(
        functools.partial(kernel, depth),
        out_shape=jax.ShapeDtypeStruct((tok_rows, width), bf16),
        in_specs=[pl.BlockSpec(memory_space=pltpu.SMEM)] * 2 + [there] * 7,
        out_specs=local,
        scratch_shapes=scratch,
        compiler_params=pltpu.CompilerParams(
            collective_id=0, has_side_effects=True, vmem_limit_bytes=63_000_000
        ),
    )(
        modality,
        expert,
        residual_in,
        context,
        out_weight,
        norm_gain.reshape(width // 128, 128),
        router,
        up_weight.reshape(width, hidden_units),
        down_weight.reshape(hidden_units, width),
    )


def solution(mesh):
    in_specs = (
        P(("role", "exp", "tp"), None),
        P(("role", "exp"), "tp"),
        P("tp", ("role", "exp")),
        P(),
        P(),
        P("role", "exp", None, "tp"),
        P("role", "exp", "tp", None),
        P(("role", "exp", "tp")),
        P(("role", "exp", "tp")),
    )
    out_specs = P(("role", "exp", "tp"), None)
    return jax.shard_map(
        per_device, mesh=mesh, in_specs=in_specs, out_specs=out_specs, check_vma=False
    )
```
